128 devices in a mesh: context: 16 (over y, x), head: 4 (over z), doc: 2 (over core).
Axes of the slice: x: 4, y: 4, z: 4, core: 2. Of those that a mesh axis runs over, the one named last changes fastest.
Arguments:
- x_input: bfloat16 [16384, 8192], P(('doc', 'context'), 'head'), parts along dimension 0, may hold values from -6 to 6
- b_input: bfloat16 [16384, 1024], P(('doc', 'context'), 'head'), parts along dimension 0, may hold values from -6 to 6
- c_input: bfloat16 [16384, 1024], P(('doc', 'context'), 'head'), parts along dimension 0, may hold values from -6 to 6
- kernel_x: float32 [4, 8192], P(None, 'head'), may hold values from -3 to 3
- kernel_b: float32 [4, 1024], P(None, 'head'), may hold values from -3 to 3
- kernel_c: float32 [4, 1024], P(None, 'head'), may hold values from -3 to 3
- step_size: float32 [16384, 128], P(('doc', 'context'), 'head'), parts along dimension 0, may hold values from 1.2207031e-05 to 0.3, as said below
- decay_log: float32 [128], P('head'), may hold values from 0 to 0.69
- skip_gain: float32 [128], P('head'), may hold values from 0.1 to 1.9
- grad_output: bfloat16 [16384, 8192], P(('doc', 'context'), 'head'), parts along dimension 0, may hold values from -6 to 6
Outputs:
- layer_output: bfloat16 [16384, 8192], P(('doc', 'context'), 'head'), parts along dimension 0
- grad_x: bfloat16 [16384, 8192], P(('doc', 'context'), 'head'), parts along dimension 0
- grad_b: bfloat16 [16384, 1024], P(('doc', 'context'), 'head'), parts along dimension 0
- grad_c: bfloat16 [16384, 1024], P(('doc', 'context'), 'head'), parts along dimension 0
The draws below stay inside these ranges and needn't reach their ends.
There are 2 independent parts, one for each index of `doc`. The reference program is written for one: setup_inputs(seed, part) draws one part's arguments, and reference() takes and returns one part's arrays. A program takes and returns all parts, laid end to end along the dimension named above; an argument that names none is the same for every part. Nothing has to cross between parts.
Inputs may be any that keep to these rules, and one draw needn't show every extreme that they name: `step_size`: positive step sizes.
All inputs are finite; a program needn't handle non-finite values.
Results may differ from the reference program's by a relative error of at most 0.018.
Values may be sent and summed in bfloat16 or wider, within the bound.
A program may use at most 256 MiB of HBM per device.

```python
import math
import jax
import jax.numpy as jnp
from jax import lax

SPACE_HEADS = 128
HEAD_DIM = 64
STATE = 256
GROUPS = 4
CONV_WIDTH = 4
BLOCK = 128
TOK_DEV = 512
DOCUMENT_TOKENS = 8192
CHANNELS = 8192
BC_WIDTH = 1024


def draw_step_size(key, part):
    every_key = jax.random.split(key, 5)
    slow_share = 55
    slow_head = jax.random.randint(every_key[0], (SPACE_HEADS,), 0, 100) < slow_share
    base_rate = jnp.where(slow_head, 0.4 / DOCUMENT_TOKENS, 0.02)
    devices = DOCUMENT_TOKENS // TOK_DEV
    device_factor = jnp.exp(jax.random.uniform(every_key[1], (devices,), jnp.float32, -math.log(2.0), math.log(2.0)))
    device_factor = jnp.repeat(device_factor, TOK_DEV)
    token_factor = jnp.exp(jax.random.uniform(every_key[2], (DOCUMENT_TOKENS, SPACE_HEADS), jnp.float32, -math.log(2.0), math.log(2.0)))
    value_per_step = base_rate[None, :] * device_factor[:, None] * token_factor
    spike_position = jax.random.randint(every_key[3], (3,), 0, DOCUMENT_TOKENS)
    spike_row = jnp.any(jnp.arange(DOCUMENT_TOKENS)[:, None] == spike_position[None, :], axis=1)
    spike_value = 0.25 * jax.random.uniform(every_key[4], (DOCUMENT_TOKENS, SPACE_HEADS), jnp.float32, 0.8, 1.2)
    return jnp.where(spike_row[:, None], spike_value, value_per_step).astype(jnp.float32)


def block_levels(stream_key, shape, shards, smallest, largest):
    loudness = 1.0
    for dim, parts in shards:
        steps = jax.random.uniform(jax.random.fold_in(jax.random.fold_in(stream_key, 6), dim), (parts,), jnp.float32, smallest / len(shards), largest / len(shards))
        loudness = loudness * jnp.repeat(jnp.exp(steps), shape[dim] // parts).reshape((-1,) + (1,) * (len(shape) - 1 - dim))
    return loudness


def bell_draw(own_key, extent, deviation, reach, shards=(), kind=jnp.bfloat16):
    factor_of = block_levels(own_key, extent, shards, -0.22, 0.18) if shards else 1.0
    drawn = jax.random.normal(own_key, extent, jnp.float32) * deviation * factor_of
    return jnp.minimum(jnp.maximum(drawn, -reach), reach).astype(kind)


def setup_inputs(seed: int = 0, part: int = 0) -> dict:
    seeds = jax.random.split(jax.random.key(seed), 11)
    own_keys = jax.random.split(jax.random.fold_in(seeds[10], part), 11)
    x_input = bell_draw(own_keys[0], (DOCUMENT_TOKENS, CHANNELS), 1.0, 6.0, ((0, 16), (1, 4)))
    b_input = bell_draw(own_keys[1], (DOCUMENT_TOKENS, BC_WIDTH), 1.0, 6.0, ((0, 16), (1, 4)))
    c_input = bell_draw(own_keys[2], (DOCUMENT_TOKENS, BC_WIDTH), 1.0, 6.0, ((0, 16), (1, 4)))
    kernel_x = bell_draw(seeds[3], (CONV_WIDTH, CHANNELS), CONV_WIDTH ** -0.5, 3.0, ((1, 4),), jnp.float32)
    kernel_b = bell_draw(seeds[4], (CONV_WIDTH, BC_WIDTH), CONV_WIDTH ** -0.5, 3.0, ((1, 4),), jnp.float32)
    kernel_c = bell_draw(seeds[5], (CONV_WIDTH, BC_WIDTH), CONV_WIDTH ** -0.5, 3.0, ((1, 4),), jnp.float32)
    step_size = draw_step_size(jax.random.fold_in(jax.random.fold_in(seeds[10], part), 71), part)
    decay_log = jnp.clip(0.69 * jax.random.uniform(seeds[7], (SPACE_HEADS,), jnp.float32) ** block_levels(seeds[7], (SPACE_HEADS,), ((0, 4),), -0.2, 0.2), 0.0, 0.69)
    skip_gain = jnp.clip(1.0 + 0.18 * jax.random.normal(seeds[8], (SPACE_HEADS,), jnp.float32), 0.1, 1.9)
    grad_output = bell_draw(own_keys[9], (DOCUMENT_TOKENS, CHANNELS), 1.0, 6.0, ((0, 16), (1, 4)))
    return {"x_input": x_input, "b_input": b_input, "c_input": c_input, "kernel_x": kernel_x, "kernel_b": kernel_b, "kernel_c": kernel_c, "step_size": step_size, "decay_log": decay_log, "skip_gain": skip_gain, "grad_output": grad_output}


def product(form, left, right):
    return jnp.einsum(form, left.astype(jnp.float32), right.astype(jnp.float32))


def silu_slope(pre_act):
    sigmoid = jax.nn.sigmoid(pre_act)
    return sigmoid * (1.0 + pre_act * (1.0 - sigmoid))


def decay_table(cumulative):
    transposed = jnp.transpose(cumulative, (0, 2, 3, 1))
    differ = transposed[..., :, None] - transposed[..., None, :]
    positions = jnp.arange(cumulative.shape[1])
    lower_mask = positions[:, None] >= positions[None, :]
    return jnp.where(lower_mask, jnp.exp(jnp.minimum(differ, 0.0)), 0.0)


def conv_apply(padded, kernel, length):
    result = jnp.zeros((length, padded.shape[1]), jnp.float32)
    for offset in range(kernel.shape[0]):
        result = result + kernel[offset][None, :] * padded[offset:offset + length].astype(jnp.float32)
    return result


def conv_back(padded_grad, kernel, length):
    result = jnp.zeros((length, padded_grad.shape[1]), jnp.float32)
    width_k = kernel.shape[0]
    for offset in range(width_k):
        begin = width_k - 1 - offset
        result = result + kernel[offset][None, :] * padded_grad[begin:begin + length].astype(jnp.float32)
    return result


def chain_forward(block_state, block_total, initial):
    def advance(carried, pair_in):
        state_k, total_k = pair_in
        return jnp.exp(total_k)[..., None, None] * carried + state_k, carried
    return lax.scan(advance, initial, (block_state, block_total))


def chain_backward(block_adj, block_total, initial):
    def retreat(carried, pair_in):
        adj_k, total_k = pair_in
        return jnp.exp(total_k)[..., None, None] * carried + adj_k, carried
    return lax.scan(retreat, initial, (block_adj, block_total), reverse=True)


def prepare(blk_x, blk_b, blk_c, step_block, log_block, grad_block):
    cumulative = jnp.cumsum(log_block, axis=1)
    table = decay_table(cumulative)
    scores = product('nigs,njgs->ngij', blk_c, blk_b)
    mixing = (table * scores[:, :, None]).astype(jnp.bfloat16)
    scaled_x = (blk_x * step_block[..., None]).astype(jnp.bfloat16)
    block_total = cumulative[:, -1]
    to_end = jnp.exp(block_total[:, None] - cumulative)
    weighted_x = (scaled_x * to_end[..., None]).astype(jnp.bfloat16)
    block_state = product('njgap,njgs->ngaps', weighted_x, blk_b)
    growth = jnp.exp(cumulative)
    grad_weighted = (grad_block * growth[..., None]).astype(jnp.bfloat16)
    block_adj = product('nigap,nigs->ngaps', grad_weighted, blk_c)
    return (table, mixing, scaled_x, to_end, weighted_x, growth, grad_weighted, block_total, block_state, block_adj)


def finish(prepared, blk_x, blk_b, blk_c, step_block, skip_block, grad_block, starts, afters):
    table, mixing, scaled_x, to_end, weighted_x, growth, grad_weighted = prepared[:7]
    start_bf = starts.astype(jnp.bfloat16)
    after_bf = afters.astype(jnp.bfloat16)
    intra_part = product('ngaij,njgap->nigap', mixing, scaled_x)
    carried_in = growth[..., None] * product('nigs,ngaps->nigap', blk_c, start_bf)
    output = (intra_part + carried_in + skip_block[:, :, None] * blk_x.astype(jnp.float32)).astype(jnp.bfloat16)
    inner_grad = product('ngaij,nigap->njgap', mixing, grad_block)
    outer_grad = to_end[..., None] * product('njgs,ngaps->njgap', blk_b, after_bf)
    grad_act_x = step_block[..., None] * (inner_grad + outer_grad) + skip_block[:, :, None] * grad_block.astype(jnp.float32)
    pair_sum = jnp.sum(table * product('nigap,njgap->ngaij', grad_block, scaled_x), axis=2).astype(jnp.bfloat16)
    grad_act_b = product('ngij,nigs->njgs', pair_sum, blk_c) + product('njgap,ngaps->njgs', weighted_x, after_bf)
    grad_act_c = product('ngij,njgs->nigs', pair_sum, blk_b) + product('nigap,ngaps->nigs', grad_weighted, start_bf)
    return output, grad_act_x, grad_act_b, grad_act_c


def group_pass(group_items):
    blk_x, blk_b, blk_c, step_block, log_block, skip_block, grad_block = group_items
    prepared = prepare(blk_x, blk_b, blk_c, step_block, log_block, grad_block)
    block_total, block_state, block_adj = prepared[7], prepared[8], prepared[9]
    empty = jnp.zeros(block_state.shape[1:], jnp.float32)
    starts = chain_forward(block_state, block_total, empty)[1]
    afters = chain_backward(block_adj, block_total, empty)[1]
    return finish(prepared, blk_x, blk_b, blk_c, step_block, skip_block, grad_block, starts, afters)


def reference(x_input, b_input, c_input, kernel_x, kernel_b, kernel_c, step_size, decay_log, skip_gain, grad_output):
    length = x_input.shape[0]
    margin = kernel_x.shape[0] - 1
    padded_x = jnp.concatenate([jnp.zeros((margin, x_input.shape[1]), x_input.dtype), x_input], axis=0)
    padded_b = jnp.concatenate([jnp.zeros((margin, b_input.shape[1]), b_input.dtype), b_input], axis=0)
    padded_c = jnp.concatenate([jnp.zeros((margin, c_input.shape[1]), c_input.dtype), c_input], axis=0)
    pre_x = conv_apply(padded_x, kernel_x, length)
    pre_b = conv_apply(padded_b, kernel_b, length)
    pre_c = conv_apply(padded_c, kernel_c, length)
    act_x = jax.nn.silu(pre_x).astype(jnp.bfloat16)
    act_b = jax.nn.silu(pre_b).astype(jnp.bfloat16)
    act_c = jax.nn.silu(pre_c).astype(jnp.bfloat16)
    blocks = length // BLOCK
    per_group = SPACE_HEADS // GROUPS
    log_step = step_size * (-jnp.exp(decay_log))[None, :]

    def regroup(values_in, inner_dims):
        shaped = values_in.reshape((blocks, BLOCK, GROUPS) + inner_dims)
        return jnp.moveaxis(shaped, 2, 0)[:, :, :, None]

    group_items = (regroup(act_x, (per_group, HEAD_DIM)), regroup(act_b, (STATE,)), regroup(act_c, (STATE,)),
                   regroup(step_size, (per_group,)), regroup(log_step, (per_group,)),
                   skip_gain.reshape(GROUPS, 1, per_group), regroup(grad_output, (per_group, HEAD_DIM)))
    output, grad_act_x, grad_act_b, grad_act_c = lax.map(group_pass, group_items)

    def ungroup(values_in):
        return jnp.moveaxis(values_in[:, :, :, 0], 0, 2).reshape(length, -1)

    grad_pre_x = (ungroup(grad_act_x) * silu_slope(pre_x)).astype(jnp.bfloat16)
    grad_pre_b = (ungroup(grad_act_b) * silu_slope(pre_b)).astype(jnp.bfloat16)
    grad_pre_c = (ungroup(grad_act_c) * silu_slope(pre_c)).astype(jnp.bfloat16)
    tail_x = jnp.zeros((margin, grad_pre_x.shape[1]), jnp.bfloat16)
    tail_b = jnp.zeros((margin, grad_pre_b.shape[1]), jnp.bfloat16)
    grad_x = conv_back(jnp.concatenate([grad_pre_x, tail_x], axis=0), kernel_x, length).astype(jnp.bfloat16)
    grad_b = conv_back(jnp.concatenate([grad_pre_b, tail_b], axis=0), kernel_b, length).astype(jnp.bfloat16)
    grad_c = conv_back(jnp.concatenate([grad_pre_c, tail_b], axis=0), kernel_c, length).astype(jnp.bfloat16)
    return (ungroup(output), grad_x, grad_b, grad_c)
```

```python
import jax
import jax.numpy as jnp
from jax import lax
from jax.experimental import pallas as pl
from jax.experimental.pallas import tpu as pltpu
from jax.sharding import PartitionSpec as P

BLOCK = 128
NB = 4
T = 512
H = 32
W = 256
NQ = 8
ST = 256
HALO = 16
LROWS = ST + HALO
MESH = pl.DeviceIdType.MESH
F32 = jnp.float32
BF = jnp.bfloat16


def dot(a, b):
    return jnp.dot(a, b, preferred_element_type=F32)


def dot_nt(a, b):
    return lax.dot_general(a, b, (((1,), (1,)), ((), ())), preferred_element_type=F32)


def split3(v):
    hi = v.astype(BF)
    rest = v - hi.astype(F32)
    mid = rest.astype(BF)
    low = (rest - mid.astype(F32)).astype(BF)
    return hi, mid, low


def sigmoid(v):
    return 1.0 / (1.0 + jnp.exp(-v))


def tail_rows(row):
    hi, mid, low = split3(row)
    index = lax.broadcasted_iota(jnp.int32, (HALO, row.shape[1]), 0)
    zero = jnp.zeros((HALO, row.shape[1]), F32)
    full = jnp.where(
        index == 0,
        hi.astype(F32),
        jnp.where(index == 1, mid.astype(F32), jnp.where(index == 2, low.astype(F32), zero)),
    )
    return full.astype(BF)


def tail_sum(rows):
    return jnp.sum(rows.astype(F32), axis=0, keepdims=True)


def kernel(
    x_hbm, b_hbm, c_hbm, kx, kb, kc, step, dlog, skip, g_hbm,
    out_hbm, gx_hbm, gb_out, gc_out,
    xp, bp, cp, gs, cb, lh, cumt, ex, tot, ske,
    slope, growth, stte, acc_o, acc_g, sx, wx, gw, ls, la,
    gh, gpb, gpc, act_b, act_c, bt, ct, slope_b, slope_c,
    ps, sl, su, grad_b, grad_c,
    sf, sb, rf, rb, tf, tb, yf, yb, of, ob, inf, inb, rs_f, rs_b,
    in_sem, out_sem, halo_s, halo_r, ghalo_s, ghalo_r,
    f1s, f1r, b1s, b1r, yfs, yfr, ybs, ybr, f2s, f2r, b2s, b2r,
):
    me = lax.axis_index("context")
    y = me // 4
    x = me % 4
    nxt = (me + 1) % 16
    prv = (me + 15) % 16

    def remote(src, dst, s, r, peer):
        return pltpu.make_async_remote_copy(
            src_ref=src, dst_ref=dst, send_sem=s, recv_sem=r,
            device_id={"context": peer}, device_id_type=MESH,
        )

    barrier = pltpu.get_barrier_semaphore()
    peers = [nxt, prv]
    peers += [y * 4 + (x + r) % 4 for r in range(1, 4)]
    peers += [((y + r) % 4) * 4 + x for r in range(1, 4)]
    for peer in peers:
        pl.semaphore_signal(barrier, inc=1, device_id={"context": peer}, device_id_type=MESH)

    body = pl.ds(HALO, T)
    loads = [
        pltpu.make_async_copy(b_hbm, bp.at[body], in_sem.at[0]),
        pltpu.make_async_copy(c_hbm, cp.at[body], in_sem.at[1]),
        pltpu.make_async_copy(x_hbm, xp.at[body], in_sem.at[2]),
        pltpu.make_async_copy(g_hbm, gs, in_sem.at[3]),
    ]
    for load in loads:
        load.start()

    rate = -jnp.exp(dlog[...])
    lower = (
        lax.broadcasted_iota(jnp.int32, (BLOCK, BLOCK), 0)
        >= lax.broadcasted_iota(jnp.int32, (BLOCK, BLOCK), 1)
    )
    lower_f = lower.astype(F32)
    lower_b = lower_f.astype(BF)
    upper_f = (
        lax.broadcasted_iota(jnp.int32, (BLOCK, BLOCK), 0)
        <= lax.broadcasted_iota(jnp.int32, (BLOCK, BLOCK), 1)
    ).astype(F32)
    for b in range(NB):
        rows = pl.ds(b * BLOCK, BLOCK)
        step_b = step[rows, :]
        logs = split3(step_b * rate)
        cum = dot(lower_b, logs[0]) + dot(lower_b, logs[1]) + dot(lower_b, logs[2])
        pieces = split3(cum) + split3(step_b)
        lh[rows, :] = jnp.concatenate([p.astype(F32) for p in pieces], axis=1).astype(BF)
        flipped = jnp.transpose(cum)
        for q in range(NQ):
            cumt[q, 0:4, rows] = flipped[4 * q : 4 * q + 4]
    skips = split3(jnp.broadcast_to(skip[...], (16, H)))
    zero_s = jnp.zeros((16, 3 * H), F32)
    lh[pl.ds(T, 16), :] = jnp.concatenate(
        [p.astype(F32) for p in skips] + [zero_s], axis=1
    ).astype(BF)
    ps[...] = jnp.zeros_like(ps)
    grad_b[...] = jnp.zeros_like(grad_b)
    grad_c[...] = jnp.zeros_like(grad_c)

    pl.semaphore_wait(barrier, 8)

    head = pl.ds(0, HALO)
    last = pl.ds(T - HALO, HALO)
    halos = [
        remote(b_hbm.at[last], bp.at[head], halo_s.at[0], halo_r.at[0], nxt),
        remote(c_hbm.at[last], cp.at[head], halo_s.at[1], halo_r.at[1], nxt),
        remote(x_hbm.at[last], xp.at[head], halo_s.at[2], halo_r.at[2], nxt),
    ]

    @pl.when(me < 15)
    def _():
        for h in halos:
            h.start()

    @pl.when(me == 0)
    def _():
        for ref in (bp, cp, xp):
            ref[head, :] = jnp.zeros((HALO, ref.shape[1]), BF)

    for load in loads:
        load.wait()

    @pl.when(me > 0)
    def _():
        for h in halos:
            h.wait_recv()

    def conv(ref, lanes, taps):
        cb[...] = ref[:, lanes].astype(F32)
        pre = taps[0:1] * cb[pl.ds(13, T), :]
        for k in range(1, 4):
            pre = pre + taps[k : k + 1] * cb[pl.ds(13 + k, T), :]
        return pre

    all_bc = pl.ds(0, ST)
    for ref, taps, act, act_t, slo in (
        (bp, kb, act_b, bt, slope_b),
        (cp, kc, act_c, ct, slope_c),
    ):
        pre = conv(ref, all_bc, taps[...])
        sig = sigmoid(pre)
        slo[...] = sig * (1.0 + pre * (1.0 - sig))
        value = (pre * sig).astype(BF)
        act[...] = value
        for b in range(NB):
            act_t[b] = jnp.transpose(value[b * BLOCK : (b + 1) * BLOCK].astype(F32)).astype(BF)
    for b in range(NB):
        rows = pl.ds(b * BLOCK, BLOCK)
        scores = dot_nt(act_c[rows, :], act_b[rows, :])
        sl[b] = scores * lower_f
        su[b] = jnp.transpose(scores) * upper_f

    def blk(b):
        return pl.ds(b * BLOCK, BLOCK)

    def lanes_of(q):
        return pl.ds(pl.multiple_of(q * W, W), W)

    def order(p):
        r = (p % 4 + 1) % 4
        k = p // 4
        return r, k, ((x + r) % 4) * 2 + k

    def row_peer(r):
        return y * 4 + (x + r) % 4

    def f1(r, k):
        return remote(
            sf.at[((x + r) % 4) * 2 + k], rf.at[x * 2 + k], f1s.at[r, k], f1r.at[r, k], row_peer(r)
        )

    def b1(r, k):
        return remote(
            sb.at[((x + r) % 4) * 2 + k], rb.at[x * 2 + k], b1s.at[r, k], b1r.at[r, k], row_peer(r)
        )

    def f2(r, k):
        return remote(
            of.at[((x + r) % 4) * 2 + k], inf.at[x * 2 + k], f2s.at[r, k], f2r.at[r, k], row_peer(r)
        )

    def b2(r, k):
        return remote(
            ob.at[((x + r) % 4) * 2 + k], inb.at[x * 2 + k], b2s.at[r, k], b2r.at[r, k], row_peer(r)
        )

    def yf_cp(r, k):
        return remote(
            tf.at[k], yf.at[y * 2 + k], yfs.at[r, k], yfr.at[y, k], ((y + r) % 4) * 4 + x
        )

    def yb_cp(r, k):
        return remote(
            tb.at[k], yb.at[y * 2 + k], ybs.at[r, k], ybr.at[y, k], ((y + r) % 4) * 4 + x
        )

    def forward_local(p, carry):
        r, k, q = order(p)
        lanes = lanes_of(q)
        depth = lax.broadcasted_iota(jnp.int32, (6 * H, 2 * W), 0)
        col = lax.broadcasted_iota(jnp.int32, (6 * H, 2 * W), 1)
        hit = (depth % H == 4 * q + (col % W) // 64) & ((depth // (3 * H)) == (col // W))
        ex[...] = dot(lh[...], hit.astype(F32).astype(BF))
        ske[q] = ex[pl.ds(T, 8), 0:W]
        pre = conv(xp, lanes, kx[:, lanes])
        sig = sigmoid(pre)
        slope[q] = sig * (1.0 + pre * (1.0 - sig))
        act = (pre * sig).astype(BF).astype(F32)
        cum = ex[pl.ds(0, T), 0:W]
        steps = ex[pl.ds(0, T), W : 2 * W]
        acc_o[q] = act * ex[pl.ds(T, 1), 0:W]
        acc_g[q] = steps
        growth[q] = jnp.exp(cum)
        scaled = (act * steps).astype(BF)
        sx[q] = scaled
        state = None
        total = None
        for b in range(NB):
            tot_b = ex[pl.ds(b * BLOCK + BLOCK - 1, 1), 0:W]
            tot[q, pl.ds(b, 1), :] = tot_b
            to_end = jnp.exp(tot_b - ex[blk(b), 0:W])
            stte[q, blk(b), :] = ex[blk(b), W : 2 * W] * to_end
            weighted = (scaled[b * BLOCK : (b + 1) * BLOCK].astype(F32) * to_end).astype(BF)
            wx[q, blk(b), :] = weighted
            grown = dot(bt[b], weighted)
            if b == 0:
                state, total = grown, tot_b
            else:
                ls[q, b - 1] = state
                state = jnp.exp(tot_b) * state + grown
                total = total + tot_b
        state = state.astype(BF)
        tail = tail_rows(total)

        @pl.when(r == 0)
        def _():
            rf[q, 0:ST, :] = state
            rf[q, ST:LROWS, :] = tail

        @pl.when(r > 0)
        def _():
            sf[q, 0:ST, :] = state
            sf[q, ST:LROWS, :] = tail
            f1(r, k).start()

        return carry

    lax.fori_loop(0, NQ, forward_local, 0)

    def backward_local(p, carry):
        r, k, q = order(p)
        lanes = lanes_of(q)
        state = None
        for b in reversed(range(NB)):
            grads = (gs[blk(b), lanes].astype(F32) * growth[q, blk(b), :]).astype(BF)
            gw[q, blk(b), :] = grads
            grown = dot(ct[b], grads)
            if b == NB - 1:
                state = jnp.exp(tot[q, pl.ds(b, 1), :]) * 0.0 + grown
            else:
                la[q, b] = state
                state = jnp.exp(tot[q, pl.ds(b, 1), :]) * state + grown
        state = state.astype(BF)

        @pl.when(r == 0)
        def _():
            rb[q] = state

        @pl.when(r > 0)
        def _():
            sb[q] = state
            b1(r, k).start()

        return carry

    lax.fori_loop(0, NQ, backward_local, 0)

    left = lax.broadcasted_iota(jnp.int32, (BLOCK, BLOCK), 1) < 64

    def halves(value):
        zero = jnp.zeros_like(value)
        return jnp.concatenate([jnp.where(left, value, zero), jnp.where(left, zero, value)], axis=0)

    def intra(q, carry):
        depth = lax.broadcasted_iota(jnp.int32, (6 * H, 2 * W), 0)
        col = lax.broadcasted_iota(jnp.int32, (6 * H, 2 * W), 1)
        hit = (depth % H == 4 * q + col // BLOCK) & (depth < 3 * H)
        hit = hit.astype(F32).astype(BF)
        for b in range(NB):
            down = dot(lh[blk(b), :], hit)
            for pair in range(2):
                part = pl.ds(pair * BLOCK, BLOCK)
                across = jnp.concatenate(
                    [cumt[q, pl.ds(2 * pair + i, 1), blk(b)] for i in range(2)], axis=1
                )
                differ = down[:, pair * W : (pair + 1) * W] - across
                table = jnp.exp(-jnp.abs(differ))
                scores = jnp.concatenate([sl[b], sl[b]], axis=1)
                scores_t = jnp.concatenate([su[b], su[b]], axis=1)
                mixing = (table * scores).astype(BF)
                mixing_t = (table * scores_t).astype(BF)
                scaled = sx[q, blk(b), part]
                grads = gs[blk(b), pl.ds(pl.multiple_of(q * W + pair * BLOCK, BLOCK), BLOCK)]
                wide_x = halves(scaled)
                acc_o[q, blk(b), part] += dot(mixing, wide_x)
                inner = dot(mixing_t, halves(grads))
                acc_g[q, blk(b), part] = (
                    acc_g[q, blk(b), part] * inner + ske[q, 0:1, part] * grads.astype(F32)
                )
                both = table * dot_nt(grads, wide_x)
                ps[b] += both[:, :BLOCK] + both[:, BLOCK:]
        return carry

    def row_forward(k):
        state, total = None, None
        for i in range(4):
            local = rf[i * 2 + k, 0:ST, :].astype(F32)
            own = tail_sum(rf[i * 2 + k, ST:LROWS, :])
            if i == 0:
                state, total = local, own
            else:
                state = jnp.exp(own) * state + local
                total = total + own
        tf[k, 0:ST, :] = state.astype(BF)
        tf[k, ST:LROWS, :] = tail_rows(total)
        rs_f[k] = jnp.zeros((ST, W), F32)
        for r in range(1, 4):
            @pl.when(y + r <= 3)
            def _():
                yf_cp(r, k).start()

    def row_backward(k):
        state = None
        for i in reversed(range(4)):
            local = rb[i * 2 + k].astype(F32)
            own = tail_sum(rf[i * 2 + k, ST:LROWS, :])
            state = local if i == 3 else jnp.exp(own) * state + local
        tb[k, 0:ST, :] = state.astype(BF)
        tb[k, ST:LROWS, :] = tf[k, ST:LROWS, :]
        rs_b[k] = jnp.zeros((ST, W), F32)
        for r in range(1, 4):
            @pl.when(y - (4 - r) >= 0)
            def _():
                yb_cp(r, k).start()

    def finish_forward(k):
        for i in range(3):
            @pl.when(i < y)
            def _():
                remote(
                    tf.at[k], yf.at[i * 2 + k], yfs.at[1, k], yfr.at[i, k], nxt
                ).wait_recv()
                own = tail_sum(yf[i * 2 + k, ST:LROWS, :])
                rs_f[k] = jnp.exp(own) * rs_f[k] + yf[i * 2 + k, 0:ST, :].astype(F32)
        state = rs_f[k]
        for i in range(4):
            out = state.astype(BF)
            of[i * 2 + k] = out

            @pl.when(x == i)
            def _():
                inf[i * 2 + k] = out

            if i < 3:
                own = tail_sum(rf[i * 2 + k, ST:LROWS, :])
                state = jnp.exp(own) * state + rf[i * 2 + k, 0:ST, :].astype(F32)
        for r in range(1, 4):
            f2(r, k).start()

    def finish_backward(k):
        for i in reversed(range(1, 4)):
            @pl.when(i > y)
            def _():
                remote(
                    tb.at[k], yb.at[i * 2 + k], ybs.at[1, k], ybr.at[i, k], nxt
                ).wait_recv()
                own = tail_sum(yb[i * 2 + k, ST:LROWS, :])
                rs_b[k] = jnp.exp(own) * rs_b[k] + yb[i * 2 + k, 0:ST, :].astype(F32)
        state = rs_b[k]
        for i in reversed(range(4)):
            out = state.astype(BF)
            ob[i * 2 + k] = out

            @pl.when(x == i)
            def _():
                inb[i * 2 + k] = out

            if i > 0:
                own = tail_sum(rf[i * 2 + k, ST:LROWS, :])
                state = jnp.exp(own) * state + rb[i * 2 + k].astype(F32)
        for r in range(1, 4):
            b2(r, k).start()

    lax.fori_loop(0, 3, intra, 0)
    for k in range(2):
        for r in range(1, 4):
            f1(r, k).wait_recv()
        row_forward(k)
    lax.fori_loop(3, 7, intra, 0)
    for k in range(2):
        finish_forward(k)
    for k in range(2):
        for r in range(1, 4):
            b1(r, k).wait_recv()
        row_backward(k)
    lax.fori_loop(7, 8, intra, 0)
    for k in range(2):
        finish_backward(k)

    def order_in(p):
        r = p % 4
        k = p // 4
        return r, k, ((x + 4 - r) % 4) * 2 + k

    def out_copy(q):
        return pltpu.make_async_copy(sx.at[q], out_hbm.at[:, lanes_of(q)], out_sem.at[0, q])

    def gx_copy(q):
        return pltpu.make_async_copy(wx.at[q], gx_hbm.at[:, lanes_of(q)], out_sem.at[1, q])

    def enter_forward(p, carry):
        r, k, q = order_in(p)

        @pl.when(r > 0)
        def _():
            f2(r, k).wait_recv()

        start = inf[q]
        base = start.astype(F32)
        total = None
        for b in range(NB):
            if b > 0:
                tot_b = tot[q, pl.ds(b - 1, 1), :]
                total = tot_b if b == 1 else total + tot_b
                start = (ls[q, b - 1] + jnp.exp(total) * base).astype(BF)
            carried = growth[q, blk(b), :] * dot(act_c[blk(b), :], start)
            sx[q, blk(b), :] = (acc_o[q, blk(b), :] + carried).astype(BF)
            grad_c[blk(b), :] += dot_nt(gw[q, blk(b), :], start)
        out_copy(q).start()
        return carry

    lax.fori_loop(0, NQ, enter_forward, 0)

    def back_conv(value, halo, taps):
        cb[pl.ds(0, T), :] = value
        cb[pl.ds(T, HALO), :] = halo
        grad = taps[0:1] * cb[pl.ds(3, T), :]
        for k in range(1, 4):
            grad = grad + taps[k : k + 1] * cb[pl.ds(3 - k, T), :]
        return grad.astype(BF)

    tail = pl.ds(T, HALO)

    def ghalo(src, dst, slot):
        return remote(src, dst, ghalo_s.at[slot], ghalo_r.at[slot], prv)

    def ghalo_x(q):
        return ghalo(gs.at[head, lanes_of(q)], gh.at[q], q)

    def ghalo_b():
        return ghalo(gpb.at[head], gpb.at[tail], NQ)

    def ghalo_c():
        return ghalo(gpc.at[head], gpc.at[tail], NQ + 1)

    def send_halo(copy):
        @pl.when(me > 0)
        def _():
            copy.start()

    def take_halo(copy, dst):
        @pl.when(me < 15)
        def _():
            copy.wait_recv()

        @pl.when(me == 15)
        def _():
            dst[...] = jnp.zeros((HALO, W), BF)

    def finish_x(p):
        q = order_in(p)[2]
        take_halo(ghalo_x(q), gh.at[q])
        wx[q] = back_conv(gs[:, lanes_of(q)].astype(F32), gh[q].astype(F32), kx[:, lanes_of(q)])
        gx_copy(q).start()

    def enter_backward(p, carry):
        r, k, q = order_in(p)

        @pl.when(r > 0)
        def _():
            b2(r, k).wait_recv()

        after = inb[q]
        base = after.astype(F32)
        total = None
        for b in reversed(range(NB)):
            if b < NB - 1:
                tot_b = tot[q, pl.ds(b + 1, 1), :]
                total = tot_b if b == NB - 2 else total + tot_b
                after = (la[q, b] + jnp.exp(total) * base).astype(BF)
            outer = stte[q, blk(b), :] * dot(act_b[blk(b), :], after)
            grads = (acc_g[q, blk(b), :] + outer) * slope[q, blk(b), :]
            gs[blk(b), lanes_of(q)] = grads.astype(BF)
            grad_b[blk(b), :] += dot_nt(wx[q, blk(b), :], after)
        send_halo(ghalo_x(q))

        @pl.when(p > 0)
        def _():
            finish_x(p - 1)

        return carry

    lax.fori_loop(0, NQ, enter_backward, 0)

    for b in range(NB):
        pair_sum = ps[b] * lower_f
        pair_t = jnp.transpose(pair_sum).astype(BF)
        pair_sum = pair_sum.astype(BF)
        into_b = grad_b[blk(b), :] + dot(pair_t, act_c[blk(b), :])
        into_c = grad_c[blk(b), :] + dot(pair_sum, act_b[blk(b), :])
        gpb[blk(b), :] = (into_b * slope_b[blk(b), :]).astype(BF)
        gpc[blk(b), :] = (into_c * slope_c[blk(b), :]).astype(BF)
    send_halo(ghalo_b())
    send_halo(ghalo_c())
    finish_x(NQ - 1)
    for ref, taps, out, copy in ((gpb, kb, gb_out, ghalo_b()), (gpc, kc, gc_out, ghalo_c())):
        take_halo(copy, ref.at[tail])
        out[...] = back_conv(
            ref[pl.ds(0, T), :].astype(F32), ref[tail, :].astype(F32), taps[...]
        )

    for q in range(NQ):
        out_copy(q).wait()
        gx_copy(q).wait()

    @pl.when(me < 15)
    def _():
        for h in halos:
            h.wait_send()

    @pl.when(me > 0)
    def _():
        for q in range(NQ):
            ghalo_x(q).wait_send()
        ghalo_b().wait_send()
        ghalo_c().wait_send()

    for k in range(2):
        for r in range(1, 4):
            f1(r, k).wait_send()
            b1(r, k).wait_send()
            f2(r, k).wait_send()
            b2(r, k).wait_send()

            @pl.when(y + r <= 3)
            def _():
                yf_cp(r, k).wait_send()

            @pl.when(y - (4 - r) >= 0)
            def _():
                yb_cp(r, k).wait_send()


def on_device(x, b, c, kx, kb, kc, step, dlog, skip, g):
    hbm = pl.BlockSpec(memory_space=pl.ANY)
    vmem = pl.BlockSpec(memory_space=pltpu.VMEM)
    dma = pltpu.SemaphoreType.DMA
    full = (NQ, T, W)
    scratch = [
        pltpu.VMEM((T + HALO, NQ * W), BF),
        pltpu.VMEM((T + HALO, ST), BF),
        pltpu.VMEM((T + HALO, ST), BF),
        pltpu.VMEM((T, NQ * W), BF),
        pltpu.VMEM((T + HALO, W), F32),
        pltpu.VMEM((T + 16, 6 * H), BF),
        pltpu.VMEM((NQ, 8, T), F32),
        pltpu.VMEM((T + 16, 2 * W), F32),
        pltpu.VMEM((NQ, 8, W), F32),
        pltpu.VMEM((NQ, 8, W), F32),
        pltpu.VMEM(full, F32),
        pltpu.VMEM(full, F32),
        pltpu.VMEM(full, F32),
        pltpu.VMEM(full, F32),
        pltpu.VMEM(full, F32),
        pltpu.VMEM(full, BF),
        pltpu.VMEM(full, BF),
        pltpu.VMEM(full, BF),
        pltpu.VMEM((NQ, 3, ST, W), F32),
        pltpu.VMEM((NQ, 3, ST, W), F32),
        pltpu.VMEM((NQ, HALO, W), BF),
        pltpu.VMEM((T + HALO, ST), BF),
        pltpu.VMEM((T + HALO, ST), BF),
        pltpu.VMEM((T, ST), BF),
        pltpu.VMEM((T, ST), BF),
        pltpu.VMEM((NB, ST, BLOCK), BF),
        pltpu.VMEM((NB, ST, BLOCK), BF),
        pltpu.VMEM((T, ST), F32),
        pltpu.VMEM((T, ST), F32),
        pltpu.VMEM((NB, BLOCK, BLOCK), F32),
        pltpu.VMEM((NB, BLOCK, BLOCK), F32),
        pltpu.VMEM((NB, BLOCK, BLOCK), F32),
        pltpu.VMEM((T, ST), F32),
        pltpu.VMEM((T, ST), F32),
        pltpu.VMEM((NQ, LROWS, W), BF),
        pltpu.VMEM((NQ, ST, W), BF),
        pltpu.VMEM((NQ, LROWS, W), BF),
        pltpu.VMEM((NQ, ST, W), BF),
        pltpu.VMEM((2, LROWS, W), BF),
        pltpu.VMEM((2, LROWS, W), BF),
        pltpu.VMEM((NQ, LROWS, W), BF),
        pltpu.VMEM((NQ, LROWS, W), BF),
        pltpu.VMEM((NQ, ST, W), BF),
        pltpu.VMEM((NQ, ST, W), BF),
        pltpu.VMEM((NQ, ST, W), BF),
        pltpu.VMEM((NQ, ST, W), BF),
        pltpu.VMEM((2, ST, W), F32),
        pltpu.VMEM((2, ST, W), F32),
        dma((4,)), dma((2, NQ)), dma((3,)), dma((3,)), dma((10,)), dma((10,)),
    ] + [dma((4, 2))] * 12
    return pl.pallas_call(
        kernel,
        out_shape=(
            jax.ShapeDtypeStruct(x.shape, BF),
            jax.ShapeDtypeStruct(x.shape, BF),
            jax.ShapeDtypeStruct(b.shape, BF),
            jax.ShapeDtypeStruct(c.shape, BF),
        ),
        in_specs=[hbm] * 3 + [vmem] * 6 + [hbm],
        out_specs=(hbm, hbm, vmem, vmem),
        scratch_shapes=scratch,
        compiler_params=pltpu.CompilerParams(
            collective_id=0, has_side_effects=True, vmem_limit_bytes=67043328
        ),
    )(x, b, c, kx, kb, kc, step, dlog.reshape(1, H), skip.reshape(1, H), g)


def solution(mesh):
    rows = P(("doc", "context"), "head")
    taps = P(None, "head")
    return jax.shard_map(
        on_device,
        mesh=mesh,
        in_specs=(rows, rows, rows, taps, taps, taps, rows, P("head"), P("head"), rows),
        out_specs=(rows, rows, rows, rows),
        check_vma=False,
    )
```

```python
import jax
import jax.numpy as jnp
from jax import lax
from jax.experimental import pallas as pl
from jax.experimental.pallas import tpu as pltpu
from jax.sharding import PartitionSpec as P

BLOCK = 128
NB = 4
T = 512
H = 32
W = 256
NQ = 8
ST = 256
HALO = 16
LROWS = ST + HALO
MESH = pl.DeviceIdType.MESH
F32 = jnp.float32
BF = jnp.bfloat16


def dot(a, b):
    return jnp.dot(a, b, preferred_element_type=F32)


def dot_nt(a, b):
    return lax.dot_general(a, b, (((1,), (1,)), ((), ())), preferred_element_type=F32)


def split3(v):
    hi = v.astype(BF)
    rest = v - hi.astype(F32)
    mid = rest.astype(BF)
    low = (rest - mid.astype(F32)).astype(BF)
    return hi, mid, low


def sigmoid(v):
    return 1.0 / (1.0 + jnp.exp(-v))


def tail_rows(row):
    hi, mid, low = split3(row)
    index = lax.broadcasted_iota(jnp.int32, (HALO, row.shape[1]), 0)
    zero = jnp.zeros((HALO, row.shape[1]), F32)
    full = jnp.where(
        index == 0,
        hi.astype(F32),
        jnp.where(index == 1, mid.astype(F32), jnp.where(index == 2, low.astype(F32), zero)),
    )
    return full.astype(BF)


def tail_sum(rows):
    return jnp.sum(rows.astype(F32), axis=0, keepdims=True)


def kernel(
    x_hbm, b_hbm, c_hbm, kx, kb, kc, step, dlog, skip, g_hbm,
    out_hbm, gp_hbm, gh_out, gpb_out, gpc_out,
    xp, bp, cp, gs, cb, lh, cumt, ex, tot, ske,
    slope, growth, stte, acc_o, acc_g, sx, wx, gw, ls, la,
    gh, gpb, gpc, act_b, act_c, bt, ct, slope_b, slope_c,
    ps, sl, su, grad_b, grad_c,
    sf, sb, rf, rb, tf, tb, yf, yb, of, ob, inf, inb, rs_f, rs_b,
    in_sem, out_sem, halo_s, halo_r, ghalo_s, ghalo_r,
    f1s, f1r, b1s, b1r, yfs, yfr, ybs, ybr, f2s, f2r, b2s, b2r,
):
    me = lax.axis_index("context")
    y = me // 4
    x = me % 4
    nxt = (me + 1) % 16
    prv = (me + 15) % 16

    def remote(src, dst, s, r, peer):
        return pltpu.make_async_remote_copy(
            src_ref=src, dst_ref=dst, send_sem=s, recv_sem=r,
            device_id={"context": peer}, device_id_type=MESH,
        )

    barrier = pltpu.get_barrier_semaphore()
    peers = [nxt, prv]
    peers += [y * 4 + (x + r) % 4 for r in range(1, 4)]
    peers += [((y + r) % 4) * 4 + x for r in range(1, 4)]
    for peer in peers:
        pl.semaphore_signal(barrier, inc=1, device_id={"context": peer}, device_id_type=MESH)

    body = pl.ds(HALO, T)
    loads = [
        pltpu.make_async_copy(b_hbm, bp.at[body], in_sem.at[0]),
        pltpu.make_async_copy(c_hbm, cp.at[body], in_sem.at[1]),
        pltpu.make_async_copy(x_hbm, xp.at[body], in_sem.at[2]),
        pltpu.make_async_copy(g_hbm, gs, in_sem.at[3]),
    ]
    for load in loads:
        load.start()

    rate = -jnp.exp(jnp.transpose(jnp.broadcast_to(dlog[...], (8, H)))[:, 0:1])
    lower = (
        lax.broadcasted_iota(jnp.int32, (BLOCK, BLOCK), 0)
        >= lax.broadcasted_iota(jnp.int32, (BLOCK, BLOCK), 1)
    )
    lower_f = lower.astype(F32)
    upper_f = (
        lax.broadcasted_iota(jnp.int32, (BLOCK, BLOCK), 0)
        <= lax.broadcasted_iota(jnp.int32, (BLOCK, BLOCK), 1)
    ).astype(F32)
    upper_b = upper_f.astype(BF)
    for b in range(NB):
        rows = pl.ds(b * BLOCK, BLOCK)
        step_b = step[:, rows]
        logs = split3(step_b * rate)
        flipped = dot(logs[0], upper_b) + dot(logs[1], upper_b) + dot(logs[2], upper_b)
        for q in range(NQ):
            cumt[q, 0:4, rows] = flipped[4 * q : 4 * q + 4]
        pieces = split3(jnp.transpose(flipped)) + split3(jnp.transpose(step_b))
        lh[rows, :] = jnp.concatenate([p.astype(F32) for p in pieces], axis=1).astype(BF)
    skips = split3(jnp.broadcast_to(skip[...], (16, H)))
    zero_s = jnp.zeros((16, 3 * H), F32)
    lh[pl.ds(T, 16), :] = jnp.concatenate(
        [p.astype(F32) for p in skips] + [zero_s], axis=1
    ).astype(BF)
    ps[...] = jnp.zeros_like(ps)
    grad_b[...] = jnp.zeros_like(grad_b)
    grad_c[...] = jnp.zeros_like(grad_c)

    pl.semaphore_wait(barrier, 8)

    head = pl.ds(0, HALO)
    last = pl.ds(T - HALO, HALO)
    halos = [
        remote(b_hbm.at[last], bp.at[head], halo_s.at[0], halo_r.at[0], nxt),
        remote(c_hbm.at[last], cp.at[head], halo_s.at[1], halo_r.at[1], nxt),
        remote(x_hbm.at[last], xp.at[head], halo_s.at[2], halo_r.at[2], nxt),
    ]

    @pl.when(me < 15)
    def _():
        for h in halos:
            h.start()

    @pl.when(me == 0)
    def _():
        for ref in (bp, cp, xp):
            ref[head, :] = jnp.zeros((HALO, ref.shape[1]), BF)

    for load in loads:
        load.wait()

    @pl.when(me > 0)
    def _():
        for h in halos:
            h.wait_recv()

    def conv(ref, lanes, taps):
        cb[...] = ref[:, lanes].astype(F32)
        pre = taps[0:1] * cb[pl.ds(13, T), :]
        for k in range(1, 4):
            pre = pre + taps[k : k + 1] * cb[pl.ds(13 + k, T), :]
        return pre

    all_bc = pl.ds(0, ST)
    for ref, taps, act, act_t, slo in (
        (bp, kb, act_b, bt, slope_b),
        (cp, kc, act_c, ct, slope_c),
    ):
        pre = conv(ref, all_bc, taps[...])
        sig = sigmoid(pre)
        slo[...] = sig * (1.0 + pre * (1.0 - sig))
        value = (pre * sig).astype(BF)
        act[...] = value
        for b in range(NB):
            act_t[b] = jnp.transpose(value[b * BLOCK : (b + 1) * BLOCK].astype(F32)).astype(BF)
    for b in range(NB):
        rows = pl.ds(b * BLOCK, BLOCK)
        scores = dot_nt(act_c[rows, :], act_b[rows, :])
        sl[b] = scores * lower_f
        su[b] = jnp.transpose(scores) * upper_f

    def blk(b):
        return pl.ds(b * BLOCK, BLOCK)

    def lanes_of(q):
        return pl.ds(pl.multiple_of(q * W, W), W)

    def order(p):
        r = (p % 4 + 1) % 4
        k = p // 4
        return r, k, ((x + r) % 4) * 2 + k

    def row_peer(r):
        return y * 4 + (x + r) % 4

    def f1(r, k):
        return remote(
            sf.at[((x + r) % 4) * 2 + k], rf.at[x * 2 + k], f1s.at[r, k], f1r.at[r, k], row_peer(r)
        )

    def b1(r, k):
        return remote(
            sb.at[((x + r) % 4) * 2 + k], rb.at[x * 2 + k], b1s.at[r, k], b1r.at[r, k], row_peer(r)
        )

    def f2(r, k):
        return remote(
            of.at[((x + r) % 4) * 2 + k], inf.at[x * 2 + k], f2s.at[r, k], f2r.at[r, k], row_peer(r)
        )

    def b2(r, k):
        return remote(
            ob.at[((x + r) % 4) * 2 + k], inb.at[x * 2 + k], b2s.at[r, k], b2r.at[r, k], row_peer(r)
        )

    def yf_cp(r, k):
        return remote(
            tf.at[k], yf.at[y * 2 + k], yfs.at[r, k], yfr.at[y, k], ((y + r) % 4) * 4 + x
        )

    def yb_cp(r, k):
        return remote(
            tb.at[k], yb.at[y * 2 + k], ybs.at[r, k], ybr.at[y, k], ((y + r) % 4) * 4 + x
        )

    def forward_local(p, carry):
        r, k, q = order(p)
        lanes = lanes_of(q)
        depth = lax.broadcasted_iota(jnp.int32, (6 * H, 2 * W), 0)
        col = lax.broadcasted_iota(jnp.int32, (6 * H, 2 * W), 1)
        hit = (depth % H == 4 * q + (col % W) // 64) & ((depth // (3 * H)) == (col // W))
        ex[...] = dot(lh[...], hit.astype(F32).astype(BF))
        ske[q] = ex[pl.ds(T, 8), 0:W]
        pre = conv(xp, lanes, kx[:, lanes])
        sig = sigmoid(pre)
        slope[q] = sig * (1.0 + pre * (1.0 - sig))
        act = (pre * sig).astype(BF).astype(F32)
        cum = ex[pl.ds(0, T), 0:W]
        steps = ex[pl.ds(0, T), W : 2 * W]
        acc_o[q] = act * ex[pl.ds(T, 1), 0:W]
        acc_g[q] = steps
        growth[q] = jnp.exp(cum)
        scaled = (act * steps).astype(BF)
        sx[q] = scaled
        state = None
        total = None
        for b in range(NB):
            tot_b = ex[pl.ds(b * BLOCK + BLOCK - 1, 1), 0:W]
            tot[q, pl.ds(b, 1), :] = tot_b
            to_end = jnp.exp(tot_b - ex[blk(b), 0:W])
            stte[q, blk(b), :] = ex[blk(b), W : 2 * W] * to_end
            weighted = (scaled[b * BLOCK : (b + 1) * BLOCK].astype(F32) * to_end).astype(BF)
            wx[q, blk(b), :] = weighted
            grown = dot(bt[b], weighted)
            if b == 0:
                state, total = grown, tot_b
            else:
                ls[q, b - 1] = state
                state = jnp.exp(tot_b) * state + grown
                total = total + tot_b
        state = state.astype(BF)
        tail = tail_rows(total)

        @pl.when(r == 0)
        def _():
            rf[q, 0:ST, :] = state
            rf[q, ST:LROWS, :] = tail

        @pl.when(r > 0)
        def _():
            sf[q, 0:ST, :] = state
            sf[q, ST:LROWS, :] = tail
            f1(r, k).start()

        return carry

    lax.fori_loop(0, NQ, forward_local, 0)

    def backward_local(p, carry):
        r, k, q = order(p)
        lanes = lanes_of(q)
        state = None
        for b in reversed(range(NB)):
            grads = (gs[blk(b), lanes].astype(F32) * growth[q, blk(b), :]).astype(BF)
            gw[q, blk(b), :] = grads
            grown = dot(ct[b], grads)
            if b == NB - 1:
                state = jnp.exp(tot[q, pl.ds(b, 1), :]) * 0.0 + grown
            else:
                la[q, b] = state
                state = jnp.exp(tot[q, pl.ds(b, 1), :]) * state + grown
        state = state.astype(BF)

        @pl.when(r == 0)
        def _():
            rb[q] = state

        @pl.when(r > 0)
        def _():
            sb[q] = state
            b1(r, k).start()

        return carry

    lax.fori_loop(0, NQ, backward_local, 0)

    left = lax.broadcasted_iota(jnp.int32, (BLOCK, BLOCK), 1) < 64

    def halves(value):
        zero = jnp.zeros_like(value)
        return jnp.concatenate([jnp.where(left, value, zero), jnp.where(left, zero, value)], axis=0)

    def intra(q, carry):
        depth = lax.broadcasted_iota(jnp.int32, (6 * H, 2 * W), 0)
        col = lax.broadcasted_iota(jnp.int32, (6 * H, 2 * W), 1)
        hit = (depth % H == 4 * q + col // BLOCK) & (depth < 3 * H)
        hit = hit.astype(F32).astype(BF)
        for b in range(NB):
            down = dot(lh[blk(b), :], hit)
            for pair in range(2):
                part = pl.ds(pair * BLOCK, BLOCK)
                across = jnp.concatenate(
                    [cumt[q, pl.ds(2 * pair + i, 1), blk(b)] for i in range(2)], axis=1
                )
                differ = down[:, pair * W : (pair + 1) * W] - across
                table = jnp.exp(-jnp.abs(differ))
                scores = jnp.concatenate([sl[b], sl[b]], axis=1)
                scores_t = jnp.concatenate([su[b], su[b]], axis=1)
                mixing = (table * scores).astype(BF)
                mixing_t = (table * scores_t).astype(BF)
                scaled = sx[q, blk(b), part]
                grads = gs[blk(b), pl.ds(pl.multiple_of(q * W + pair * BLOCK, BLOCK), BLOCK)]
                wide_x = halves(scaled)
                acc_o[q, blk(b), part] += dot(mixing, wide_x)
                inner = dot(mixing_t, halves(grads))
                acc_g[q, blk(b), part] = (
                    acc_g[q, blk(b), part] * inner + ske[q, 0:1, part] * grads.astype(F32)
                )
                both = table * dot_nt(grads, wide_x)
                ps[b] += both[:, :BLOCK] + both[:, BLOCK:]
        return carry

    def row_forward(k):
        state, total = None, None
        for i in range(4):
            local = rf[i * 2 + k, 0:ST, :].astype(F32)
            own = tail_sum(rf[i * 2 + k, ST:LROWS, :])
            if i == 0:
                state, total = local, own
            else:
                state = jnp.exp(own) * state + local
                total = total + own
        tf[k, 0:ST, :] = state.astype(BF)
        tf[k, ST:LROWS, :] = tail_rows(total)
        rs_f[k] = jnp.zeros((ST, W), F32)
        for r in range(1, 4):
            @pl.when(y + r <= 3)
            def _():
                yf_cp(r, k).start()

    def row_backward(k):
        state = None
        for i in reversed(range(4)):
            local = rb[i * 2 + k].astype(F32)
            own = tail_sum(rf[i * 2 + k, ST:LROWS, :])
            state = local if i == 3 else jnp.exp(own) * state + local
        tb[k, 0:ST, :] = state.astype(BF)
        tb[k, ST:LROWS, :] = tf[k, ST:LROWS, :]
        rs_b[k] = jnp.zeros((ST, W), F32)
        for r in range(1, 4):
            @pl.when(y - (4 - r) >= 0)
            def _():
                yb_cp(r, k).start()

    def finish_forward(k):
        for i in range(3):
            @pl.when(i < y)
            def _():
                remote(
                    tf.at[k], yf.at[i * 2 + k], yfs.at[1, k], yfr.at[i, k], nxt
                ).wait_recv()
                own = tail_sum(yf[i * 2 + k, ST:LROWS, :])
                rs_f[k] = jnp.exp(own) * rs_f[k] + yf[i * 2 + k, 0:ST, :].astype(F32)
        state = rs_f[k]
        for i in range(4):
            out = state.astype(BF)
            of[i * 2 + k] = out

            @pl.when(x == i)
            def _():
                inf[i * 2 + k] = out

            if i < 3:
                own = tail_sum(rf[i * 2 + k, ST:LROWS, :])
                state = jnp.exp(own) * state + rf[i * 2 + k, 0:ST, :].astype(F32)
        for r in range(1, 4):
            f2(r, k).start()

    def finish_backward(k):
        for i in reversed(range(1, 4)):
            @pl.when(i > y)
            def _():
                remote(
                    tb.at[k], yb.at[i * 2 + k], ybs.at[1, k], ybr.at[i, k], nxt
                ).wait_recv()
                own = tail_sum(yb[i * 2 + k, ST:LROWS, :])
                rs_b[k] = jnp.exp(own) * rs_b[k] + yb[i * 2 + k, 0:ST, :].astype(F32)
        state = rs_b[k]
        for i in reversed(range(4)):
            out = state.astype(BF)
            ob[i * 2 + k] = out

            @pl.when(x == i)
            def _():
                inb[i * 2 + k] = out

            if i > 0:
                own = tail_sum(rf[i * 2 + k, ST:LROWS, :])
                state = jnp.exp(own) * state + rb[i * 2 + k].astype(F32)
        for r in range(1, 4):
            b2(r, k).start()

    lax.fori_loop(0, 3, intra, 0)
    for k in range(2):
        for r in range(1, 4):
            f1(r, k).wait_recv()
        row_forward(k)
    lax.fori_loop(3, 7, intra, 0)
    for k in range(2):
        finish_forward(k)
    for k in range(2):
        for r in range(1, 4):
            b1(r, k).wait_recv()
        row_backward(k)
    lax.fori_loop(7, 8, intra, 0)
    for k in range(2):
        finish_backward(k)

    def order_in(p):
        r = p % 4
        k = p // 4
        return r, k, ((x + 4 - r) % 4) * 2 + k

    def out_copy(q):
        return pltpu.make_async_copy(sx.at[q], out_hbm.at[:, lanes_of(q)], out_sem.at[0, q])

    def gp_copy(q):
        lanes = lanes_of(q)
        return pltpu.make_async_copy(gs.at[:, lanes], gp_hbm.at[:, lanes], out_sem.at[1, q])

    def enter_forward(p, carry):
        r, k, q = order_in(p)

        @pl.when(r > 0)
        def _():
            f2(r, k).wait_recv()

        start = inf[q]
        base = start.astype(F32)
        total = None
        for b in range(NB):
            if b > 0:
                tot_b = tot[q, pl.ds(b - 1, 1), :]
                total = tot_b if b == 1 else total + tot_b
                start = (ls[q, b - 1] + jnp.exp(total) * base).astype(BF)
            carried = growth[q, blk(b), :] * dot(act_c[blk(b), :], start)
            sx[q, blk(b), :] = (acc_o[q, blk(b), :] + carried).astype(BF)
            grad_c[blk(b), :] += dot_nt(gw[q, blk(b), :], start)
        out_copy(q).start()
        return carry

    lax.fori_loop(0, NQ, enter_forward, 0)

    tail = pl.ds(T, HALO)

    def ghalo(src, dst, slot):
        return remote(src, dst, ghalo_s.at[slot], ghalo_r.at[slot], prv)

    def ghalo_x(q):
        return ghalo(gs.at[head, lanes_of(q)], gh.at[q], q)

    def ghalo_b():
        return ghalo(gpb.at[head], gpb.at[tail], NQ)

    def ghalo_c():
        return ghalo(gpc.at[head], gpc.at[tail], NQ + 1)

    def send_halo(copy):
        @pl.when(me > 0)
        def _():
            copy.start()

    def take_halo(copy, dst):
        @pl.when(me < 15)
        def _():
            copy.wait_recv()

        @pl.when(me == 15)
        def _():
            dst[...] = jnp.zeros((HALO, W), BF)

    def enter_backward(p, carry):
        r, k, q = order_in(p)

        @pl.when(r > 0)
        def _():
            b2(r, k).wait_recv()

        after = inb[q]
        base = after.astype(F32)
        total = None
        for b in reversed(range(NB)):
            if b < NB - 1:
                tot_b = tot[q, pl.ds(b + 1, 1), :]
                total = tot_b if b == NB - 2 else total + tot_b
                after = (la[q, b] + jnp.exp(total) * base).astype(BF)
            outer = stte[q, blk(b), :] * dot(act_b[blk(b), :], after)
            grads = (acc_g[q, blk(b), :] + outer) * slope[q, blk(b), :]
            gs[blk(b), lanes_of(q)] = grads.astype(BF)
            grad_b[blk(b), :] += dot_nt(wx[q, blk(b), :], after)
        send_halo(ghalo_x(q))
        gp_copy(q).start()
        return carry

    lax.fori_loop(0, NQ, enter_backward, 0)

    for b in range(NB):
        pair_sum = ps[b] * lower_f
        pair_t = jnp.transpose(pair_sum).astype(BF)
        pair_sum = pair_sum.astype(BF)
        into_b = grad_b[blk(b), :] + dot(pair_t, act_c[blk(b), :])
        into_c = grad_c[blk(b), :] + dot(pair_sum, act_b[blk(b), :])
        gpb[blk(b), :] = (into_b * slope_b[blk(b), :]).astype(BF)
        gpc[blk(b), :] = (into_c * slope_c[blk(b), :]).astype(BF)
    send_halo(ghalo_b())
    send_halo(ghalo_c())
    gpb_out[pl.ds(0, T), :] = gpb[pl.ds(0, T), :]
    gpc_out[pl.ds(0, T), :] = gpc[pl.ds(0, T), :]
    for q in range(NQ):
        take_halo(ghalo_x(q), gh.at[q])
        gh_out[:, q * W : (q + 1) * W] = gh[q]
    for ref, out, copy in ((gpb, gpb_out, ghalo_b()), (gpc, gpc_out, ghalo_c())):
        take_halo(copy, ref.at[tail])
        out[tail, :] = ref[tail, :]

    for q in range(NQ):
        out_copy(q).wait()
        gp_copy(q).wait()

    @pl.when(me < 15)
    def _():
        for h in halos:
            h.wait_send()

    @pl.when(me > 0)
    def _():
        for q in range(NQ):
            ghalo_x(q).wait_send()
        ghalo_b().wait_send()
        ghalo_c().wait_send()

    for k in range(2):
        for r in range(1, 4):
            f1(r, k).wait_send()
            b1(r, k).wait_send()
            f2(r, k).wait_send()
            b2(r, k).wait_send()

            @pl.when(y + r <= 3)
            def _():
                yf_cp(r, k).wait_send()

            @pl.when(y - (4 - r) >= 0)
            def _():
                yb_cp(r, k).wait_send()


def back_kernel(out, gp, gh, gpb, gpc, kx, kb, kc, out_ref, gx_ref, gb_ref, gc_ref, cb):
    def back(taps):
        grad = taps[0:1] * cb[pl.ds(3, T), :]
        for k in range(1, 4):
            grad = grad + taps[k : k + 1] * cb[pl.ds(3 - k, T), :]
        return grad.astype(BF)

    out_ref[...] = out[...]
    cb[pl.ds(0, T), :] = gp[...].astype(F32)
    cb[pl.ds(T, HALO), :] = gh[...].astype(F32)
    gx_ref[...] = back(kx[...])

    @pl.when(pl.program_id(0) == 0)
    def _():
        for ref, taps, res in ((gpb, kb, gb_ref), (gpc, kc, gc_ref)):
            cb[...] = ref[...].astype(F32)
            res[...] = back(taps[...])


def on_device(x, b, c, kx, kb, kc, step, dlog, skip, g):
    hbm = pl.BlockSpec(memory_space=pl.ANY)
    vmem = pl.BlockSpec(memory_space=pltpu.VMEM)
    dma = pltpu.SemaphoreType.DMA
    full = (NQ, T, W)
    scratch = [
        pltpu.VMEM((T + HALO, NQ * W), BF),
        pltpu.VMEM((T + HALO, ST), BF),
        pltpu.VMEM((T + HALO, ST), BF),
        pltpu.VMEM((T, NQ * W), BF),
        pltpu.VMEM((T + HALO, W), F32),
        pltpu.VMEM((T + 16, 6 * H), BF),
        pltpu.VMEM((NQ, 8, T), F32),
        pltpu.VMEM((T + 16, 2 * W), F32),
        pltpu.VMEM((NQ, 8, W), F32),
        pltpu.VMEM((NQ, 8, W), F32),
        pltpu.VMEM(full, F32),
        pltpu.VMEM(full, F32),
        pltpu.VMEM(full, F32),
        pltpu.VMEM(full, F32),
        pltpu.VMEM(full, F32),
        pltpu.VMEM(full, BF),
        pltpu.VMEM(full, BF),
        pltpu.VMEM(full, BF),
        pltpu.VMEM((NQ, 3, ST, W), F32),
        pltpu.VMEM((NQ, 3, ST, W), F32),
        pltpu.VMEM((NQ, HALO, W), BF),
        pltpu.VMEM((T + HALO, ST), BF),
        pltpu.VMEM((T + HALO, ST), BF),
        pltpu.VMEM((T, ST), BF),
        pltpu.VMEM((T, ST), BF),
        pltpu.VMEM((NB, ST, BLOCK), BF),
        pltpu.VMEM((NB, ST, BLOCK), BF),
        pltpu.VMEM((T, ST), F32),
        pltpu.VMEM((T, ST), F32),
        pltpu.VMEM((NB, BLOCK, BLOCK), F32),
        pltpu.VMEM((NB, BLOCK, BLOCK), F32),
        pltpu.VMEM((NB, BLOCK, BLOCK), F32),
        pltpu.VMEM((T, ST), F32),
        pltpu.VMEM((T, ST), F32),
        pltpu.VMEM((NQ, LROWS, W), BF),
        pltpu.VMEM((NQ, ST, W), BF),
        pltpu.VMEM((NQ, LROWS, W), BF),
        pltpu.VMEM((NQ, ST, W), BF),
        pltpu.VMEM((2, LROWS, W), BF),
        pltpu.VMEM((2, LROWS, W), BF),
        pltpu.VMEM((NQ, LROWS, W), BF),
        pltpu.VMEM((NQ, LROWS, W), BF),
        pltpu.VMEM((NQ, ST, W), BF),
        pltpu.VMEM((NQ, ST, W), BF),
        pltpu.VMEM((NQ, ST, W), BF),
        pltpu.VMEM((NQ, ST, W), BF),
        pltpu.VMEM((2, ST, W), F32),
        pltpu.VMEM((2, ST, W), F32),
        dma((4,)), dma((2, NQ)), dma((3,)), dma((3,)), dma((10,)), dma((10,)),
    ] + [dma((4, 2))] * 12
    out, gp, gh, gpb, gpc = pl.pallas_call(
        kernel,
        out_shape=(
            jax.ShapeDtypeStruct(x.shape, BF),
            jax.ShapeDtypeStruct(x.shape, BF),
            jax.ShapeDtypeStruct((HALO, NQ * W), BF),
            jax.ShapeDtypeStruct((T + HALO, ST), BF),
            jax.ShapeDtypeStruct((T + HALO, ST), BF),
        ),
        in_specs=[hbm] * 3 + [vmem] * 6 + [hbm],
        out_specs=(hbm, hbm, vmem, vmem, vmem),
        scratch_shapes=scratch,
        compiler_params=pltpu.CompilerParams(
            collective_id=0, has_side_effects=True, vmem_limit_bytes=67043328
        ),
    )(x, b, c, kx, kb, kc, step.T, dlog.reshape(1, H), skip.reshape(1, H), g)
    slab = pl.BlockSpec((T, W), lambda q: (0, q))
    whole = pl.BlockSpec((T, ST), lambda q: (0, 0))
    padded = pl.BlockSpec((T + HALO, ST), lambda q: (0, 0))
    small = pl.BlockSpec((4, ST), lambda q: (0, 0))
    return pl.pallas_call(
        back_kernel,
        grid=(NQ,),
        out_shape=(
            jax.ShapeDtypeStruct(x.shape, BF),
            jax.ShapeDtypeStruct(x.shape, BF),
            jax.ShapeDtypeStruct(b.shape, BF),
            jax.ShapeDtypeStruct(c.shape, BF),
        ),
        in_specs=[
            slab, slab, pl.BlockSpec((HALO, W), lambda q: (0, q)), padded, padded,
            pl.BlockSpec((4, W), lambda q: (0, q)), small, small,
        ],
        out_specs=(slab, slab, whole, whole),
        scratch_shapes=[pltpu.VMEM((T + HALO, W), F32)],
    )(out, gp, gh, gpb, gpc, kx, kb, kc)


def solution(mesh):
    rows = P(("doc", "context"), "head")
    taps = P(None, "head")
    return jax.shard_map(
        on_device,
        mesh=mesh,
        in_specs=(rows, rows, rows, taps, taps, taps, rows, P("head"), P("head"), rows),
        out_specs=(rows, rows, rows, rows),
        check_vma=False,
    )
```

```python
import jax
import jax.numpy as jnp
from jax import lax
from jax.experimental import pallas as pl
from jax.experimental.pallas import tpu as pltpu
from jax.sharding import PartitionSpec as P

BLOCK = 128
NB = 4
T = 512
H = 32
W = 256
NQ = 8
ST = 256
HALO = 16
LROWS = ST + HALO
MESH = pl.DeviceIdType.MESH
F32 = jnp.float32
BF = jnp.bfloat16


def dot(a, b):
    return jnp.dot(a, b, preferred_element_type=F32)


def dot_nt(a, b):
    return lax.dot_general(a, b, (((1,), (1,)), ((), ())), preferred_element_type=F32)


def split3(v):
    hi = v.astype(BF)
    rest = v - hi.astype(F32)
    mid = rest.astype(BF)
    low = (rest - mid.astype(F32)).astype(BF)
    return hi, mid, low


def sigmoid(v):
    return 1.0 / (1.0 + jnp.exp(-v))


def tail_rows(row):
    hi, mid, low = split3(row)
    index = lax.broadcasted_iota(jnp.int32, (HALO, row.shape[1]), 0)
    zero = jnp.zeros((HALO, row.shape[1]), F32)
    full = jnp.where(
        index == 0,
        hi.astype(F32),
        jnp.where(index == 1, mid.astype(F32), jnp.where(index == 2, low.astype(F32), zero)),
    )
    return full.astype(BF)


def tail_sum(rows):
    return jnp.sum(rows.astype(F32), axis=0, keepdims=True)


def kernel(
    x_hbm, b_hbm, c_hbm, kx, kb, kc, step, dlog, skip, g_hbm,
    out_hbm, gp_hbm, gh_out, gpb_out, gpc_out,
    xp, bp, cp, gs, lh, cumt, ex, tot, ske,
    slope, growth, stte, acc_o, acc_g, sx, wx, gw, ls, la,
    gh, gpb, gpc, act_b, act_c, bt, ct, slope_b, slope_c,
    ps, sl, su, grad_b, grad_c,
    sf, sb, rf, rb, tf, tb, yf, yb, of, ob, inf, inb, rs_f, rs_b,
    in_sem, out_sem, halo_s, halo_r, ghalo_s, ghalo_r,
    f1s, f1r, b1s, b1r, yfs, yfr, ybs, ybr, f2s, f2r, b2s, b2r,
):
    me = lax.axis_index("context")
    y = me // 4
    x = me % 4
    nxt = (me + 1) % 16
    prv = (me + 15) % 16

    def remote(src, dst, s, r, peer):
        return pltpu.make_async_remote_copy(
            src_ref=src, dst_ref=dst, send_sem=s, recv_sem=r,
            device_id={"context": peer}, device_id_type=MESH,
        )

    barrier = pltpu.get_barrier_semaphore()
    peers = [nxt, prv]
    peers += [y * 4 + (x + r) % 4 for r in range(1, 4)]
    peers += [((y + r) % 4) * 4 + x for r in range(1, 4)]
    for peer in peers:
        pl.semaphore_signal(barrier, inc=1, device_id={"context": peer}, device_id_type=MESH)

    body = pl.ds(HALO, T)
    loads = [
        pltpu.make_async_copy(b_hbm, bp.at[body], in_sem.at[0]),
        pltpu.make_async_copy(c_hbm, cp.at[body], in_sem.at[1]),
        pltpu.make_async_copy(x_hbm, xp.at[body], in_sem.at[2]),
        pltpu.make_async_copy(g_hbm, gs, in_sem.at[3]),
    ]
    for load in loads:
        load.start()

    rate = -jnp.exp(jnp.transpose(jnp.broadcast_to(dlog[...], (8, H)))[:, 0:1])
    lower = (
        lax.broadcasted_iota(jnp.int32, (BLOCK, BLOCK), 0)
        >= lax.broadcasted_iota(jnp.int32, (BLOCK, BLOCK), 1)
    )
    lower_f = lower.astype(F32)
    upper_f = (
        lax.broadcasted_iota(jnp.int32, (BLOCK, BLOCK), 0)
        <= lax.broadcasted_iota(jnp.int32, (BLOCK, BLOCK), 1)
    ).astype(F32)
    upper_b = upper_f.astype(BF)
    for b in range(NB):
        rows = pl.ds(b * BLOCK, BLOCK)
        step_b = step[:, rows]
        logs = split3(step_b * rate)
        flipped = dot(logs[0], upper_b) + dot(logs[1], upper_b) + dot(logs[2], upper_b)
        for q in range(NQ):
            cumt[q, 0:4, rows] = flipped[4 * q : 4 * q + 4]
        pieces = split3(jnp.transpose(flipped)) + split3(jnp.transpose(step_b))
        lh[rows, :] = jnp.concatenate([p.astype(F32) for p in pieces], axis=1).astype(BF)
    skips = split3(jnp.broadcast_to(skip[...], (16, H)))
    zero_s = jnp.zeros((16, 3 * H), F32)
    lh[pl.ds(T, 16), :] = jnp.concatenate(
        [p.astype(F32) for p in skips] + [zero_s], axis=1
    ).astype(BF)
    ps[...] = jnp.zeros_like(ps)
    grad_c[...] = jnp.zeros_like(grad_c)

    pl.semaphore_wait(barrier, 8)

    head = pl.ds(0, HALO)
    last = pl.ds(T - HALO, HALO)
    halos = [
        remote(b_hbm.at[last], bp.at[head], halo_s.at[0], halo_r.at[0], nxt),
        remote(c_hbm.at[last], cp.at[head], halo_s.at[1], halo_r.at[1], nxt),
        remote(x_hbm.at[last], xp.at[head], halo_s.at[2], halo_r.at[2], nxt),
    ]

    @pl.when(me < 15)
    def _():
        for h in halos:
            h.start()

    @pl.when(me == 0)
    def _():
        for ref in (bp, cp, xp):
            ref[head, :] = jnp.zeros((HALO, ref.shape[1]), BF)

    def blk(b):
        return pl.ds(b * BLOCK, BLOCK)

    def lanes_of(q):
        return pl.ds(pl.multiple_of(q * W, W), W)

    def spread(q, carry):
        depth = lax.broadcasted_iota(jnp.int32, (6 * H, 2 * W), 0)
        col = lax.broadcasted_iota(jnp.int32, (6 * H, 2 * W), 1)
        hit = (depth % H == 4 * q + (col % W) // 64) & ((depth // (3 * H)) == (col // W))
        ex[...] = dot(lh[...], hit.astype(F32).astype(BF))
        ske[q] = ex[pl.ds(T, 8), 0:W]
        for b in range(NB):
            cum = ex[blk(b), 0:W]
            steps = ex[blk(b), W : 2 * W]
            tot_b = ex[pl.ds(b * BLOCK + BLOCK - 1, 1), 0:W]
            tot[q, pl.ds(b, 1), :] = tot_b
            to_end = jnp.exp(tot_b - cum)
            growth[q, blk(b), :] = jnp.exp(cum)
            acc_o[q, blk(b), :] = to_end
            acc_g[q, blk(b), :] = steps
            stte[q, blk(b), :] = steps * to_end
        return carry

    lax.fori_loop(0, NQ, spread, 0)

    for load in loads:
        load.wait()

    @pl.when(me > 0)
    def _():
        for h in halos:
            h.wait_recv()

    def conv(ref, lanes, taps):
        padded = ref[:, lanes].astype(F32)
        pre = taps[3:4] * padded[HALO:]
        for k in range(3):
            pre = pre + taps[k : k + 1] * pltpu.roll(padded, 3 - k, 0)[HALO:]
        return pre

    all_bc = pl.ds(0, ST)
    for ref, taps, act, act_t, slo in (
        (bp, kb, act_b, bt, slope_b),
        (cp, kc, act_c, ct, slope_c),
    ):
        pre = conv(ref, all_bc, taps[...])
        sig = sigmoid(pre)
        slo[...] = sig * (1.0 + pre * (1.0 - sig))
        value = (pre * sig).astype(BF)
        act[...] = value
        for b in range(NB):
            act_t[b] = jnp.transpose(value[b * BLOCK : (b + 1) * BLOCK].astype(F32)).astype(BF)
    for b in range(NB):
        rows = pl.ds(b * BLOCK, BLOCK)
        scores = dot_nt(act_c[rows, :], act_b[rows, :])
        sl[b] = scores * lower_f
        su[b] = jnp.transpose(scores) * upper_f

    def order(p):
        far = p < 6
        r = jnp.where(far, p % 3 + 1, 0)
        k = jnp.where(far, p // 3, p - 6)
        return r, k, ((x + r) % 4) * 2 + k

    def row_peer(r):
        return y * 4 + (x + r) % 4

    def f1(r, k):
        return remote(
            sf.at[((x + r) % 4) * 2 + k], rf.at[x * 2 + k], f1s.at[r, k], f1r.at[r, k], row_peer(r)
        )

    def b1(r, k):
        return remote(
            sb.at[((x + r) % 4) * 2 + k], rb.at[x * 2 + k], b1s.at[r, k], b1r.at[r, k], row_peer(r)
        )

    def f2(r, k):
        return remote(
            of.at[((x + r) % 4) * 2 + k], inf.at[x * 2 + k], f2s.at[r, k], f2r.at[r, k], row_peer(r)
        )

    def b2(r, k):
        return remote(
            ob.at[((x + r) % 4) * 2 + k], inb.at[x * 2 + k], b2s.at[r, k], b2r.at[r, k], row_peer(r)
        )

    def yf_cp(r, k):
        return remote(
            tf.at[k], yf.at[y * 2 + k], yfs.at[r, k], yfr.at[y, k], ((y + r) % 4) * 4 + x
        )

    def yb_cp(r, k):
        return remote(
            tb.at[k], yb.at[y * 2 + k], ybs.at[r, k], ybr.at[y, k], ((y + r) % 4) * 4 + x
        )

    def forward_local(p, carry):
        r, k, q = order(p)
        lanes = lanes_of(q)
        pre = conv(xp, lanes, kx[:, lanes])
        slope[q] = pre
        act = (pre * sigmoid(pre)).astype(BF).astype(F32)
        scaled = (act * acc_g[q]).astype(BF)
        sx[q] = scaled
        weighted = (scaled.astype(F32) * acc_o[q]).astype(BF)
        wx[q] = weighted
        state = None
        total = None
        for b in range(NB):
            tot_b = tot[q, pl.ds(b, 1), :]
            grown = dot(bt[b], weighted[b * BLOCK : (b + 1) * BLOCK])
            if b == 0:
                state, total = grown, tot_b
            else:
                ls[q, b - 1] = state
                state = jnp.exp(tot_b) * state + grown
                total = total + tot_b
        state = state.astype(BF)
        tail = tail_rows(total)

        @pl.when(r == 0)
        def _():
            rf[q, 0:ST, :] = state
            rf[q, ST:LROWS, :] = tail

        @pl.when(r > 0)
        def _():
            sf[q, 0:ST, :] = state
            sf[q, ST:LROWS, :] = tail
            f1(r, k).start()

        return carry

    lax.fori_loop(0, NQ, forward_local, 0)

    def backward_local(p, carry):
        r, k, q = order(p)
        lanes = lanes_of(q)
        state = None
        for b in reversed(range(NB)):
            grads = (gs[blk(b), lanes].astype(F32) * growth[q, blk(b), :]).astype(BF)
            gw[q, blk(b), :] = grads
            grown = dot(ct[b], grads)
            if b == NB - 1:
                state = grown
            else:
                la[q, b] = state
                state = jnp.exp(tot[q, pl.ds(b, 1), :]) * state + grown
        state = state.astype(BF)

        @pl.when(r == 0)
        def _():
            rb[q] = state

        @pl.when(r > 0)
        def _():
            sb[q] = state
            b1(r, k).start()

        return carry

    lax.fori_loop(0, NQ, backward_local, 0)

    left = lax.broadcasted_iota(jnp.int32, (BLOCK, BLOCK), 1) < 64

    def halves(value):
        zero = jnp.zeros_like(value)
        return jnp.concatenate([jnp.where(left, value, zero), jnp.where(left, zero, value)], axis=0)

    def intra(q, carry):
        depth = lax.broadcasted_iota(jnp.int32, (6 * H, 2 * W), 0)
        col = lax.broadcasted_iota(jnp.int32, (6 * H, 2 * W), 1)
        hit = (depth % H == 4 * q + col // BLOCK) & (depth < 3 * H)
        hit = hit.astype(F32).astype(BF)
        for b in range(NB):
            down = dot(lh[blk(b), :], hit)
            for pair in range(2):
                part = pl.ds(pair * BLOCK, BLOCK)
                across = jnp.concatenate(
                    [cumt[q, pl.ds(2 * pair + i, 1), blk(b)] for i in range(2)], axis=1
                )
                differ = down[:, pair * W : (pair + 1) * W] - across
                table = jnp.exp(-jnp.abs(differ))
                scores = jnp.concatenate([sl[b], sl[b]], axis=1)
                scores_t = jnp.concatenate([su[b], su[b]], axis=1)
                mixing = (table * scores).astype(BF)
                mixing_t = (table * scores_t).astype(BF)
                scaled = sx[q, blk(b), part]
                grads = gs[blk(b), pl.ds(pl.multiple_of(q * W + pair * BLOCK, BLOCK), BLOCK)]
                wide_x = halves(scaled)
                pre = slope[q, blk(b), part]
                sig = sigmoid(pre)
                slope[q, blk(b), part] = sig * (1.0 + pre * (1.0 - sig))
                direct = ske[q, 0:1, part] * (pre * sig).astype(BF).astype(F32)
                acc_o[q, blk(b), part] = direct + dot(mixing, wide_x)
                inner = dot(mixing_t, halves(grads))
                acc_g[q, blk(b), part] = (
                    acc_g[q, blk(b), part] * inner + ske[q, 0:1, part] * grads.astype(F32)
                )
                both = table * dot_nt(grads, wide_x)
                ps[b] += both[:, :BLOCK] + both[:, BLOCK:]
        return carry

    def row_forward(k):
        state, total = None, None
        for i in range(4):
            local = rf[i * 2 + k, 0:ST, :].astype(F32)
            own = tail_sum(rf[i * 2 + k, ST:LROWS, :])
            if i == 0:
                state, total = local, own
            else:
                state = jnp.exp(own) * state + local
                total = total + own
        tf[k, 0:ST, :] = state.astype(BF)
        tf[k, ST:LROWS, :] = tail_rows(total)
        rs_f[k] = jnp.zeros((ST, W), F32)
        for r in range(1, 4):
            @pl.when(y + r <= 3)
            def _():
                yf_cp(r, k).start()

    def row_backward(k):
        state = None
        for i in reversed(range(4)):
            local = rb[i * 2 + k].astype(F32)
            own = tail_sum(rf[i * 2 + k, ST:LROWS, :])
            state = local if i == 3 else jnp.exp(own) * state + local
        tb[k, 0:ST, :] = state.astype(BF)
        tb[k, ST:LROWS, :] = tf[k, ST:LROWS, :]
        rs_b[k] = jnp.zeros((ST, W), F32)
        for r in range(1, 4):
            @pl.when(y - (4 - r) >= 0)
            def _():
                yb_cp(r, k).start()

    def finish_forward(k):
        for i in range(3):
            @pl.when(i < y)
            def _():
                remote(
                    tf.at[k], yf.at[i * 2 + k], yfs.at[1, k], yfr.at[i, k], nxt
                ).wait_recv()
                own = tail_sum(yf[i * 2 + k, ST:LROWS, :])
                rs_f[k] = jnp.exp(own) * rs_f[k] + yf[i * 2 + k, 0:ST, :].astype(F32)
        state = rs_f[k]
        for i in range(4):
            out = state.astype(BF)
            of[i * 2 + k] = out

            @pl.when(x == i)
            def _():
                inf[i * 2 + k] = out

            if i < 3:
                own = tail_sum(rf[i * 2 + k, ST:LROWS, :])
                state = jnp.exp(own) * state + rf[i * 2 + k, 0:ST, :].astype(F32)
        for r in range(1, 4):
            f2(r, k).start()

    def finish_backward(k):
        for i in reversed(range(1, 4)):
            @pl.when(i > y)
            def _():
                remote(
                    tb.at[k], yb.at[i * 2 + k], ybs.at[1, k], ybr.at[i, k], nxt
                ).wait_recv()
                own = tail_sum(yb[i * 2 + k, ST:LROWS, :])
                rs_b[k] = jnp.exp(own) * rs_b[k] + yb[i * 2 + k, 0:ST, :].astype(F32)
        state = rs_b[k]
        for i in reversed(range(4)):
            out = state.astype(BF)
            ob[i * 2 + k] = out

            @pl.when(x == i)
            def _():
                inb[i * 2 + k] = out

            if i > 0:
                own = tail_sum(rf[i * 2 + k, ST:LROWS, :])
                state = jnp.exp(own) * state + rb[i * 2 + k].astype(F32)
        for r in range(1, 4):
            b2(r, k).start()

    lax.fori_loop(0, 3, intra, 0)
    for k in range(2):
        for r in range(1, 4):
            f1(r, k).wait_recv()
        row_forward(k)
    lax.fori_loop(3, 7, intra, 0)
    for k in range(2):
        finish_forward(k)
    for k in range(2):
        for r in range(1, 4):
            b1(r, k).wait_recv()
        row_backward(k)
    lax.fori_loop(7, 8, intra, 0)
    for k in range(2):
        finish_backward(k)

    def order_in(p):
        r = p % 4
        k = p // 4
        return r, k, ((x + 4 - r) % 4) * 2 + k

    def out_copy(q):
        return pltpu.make_async_copy(sx.at[q], out_hbm.at[:, lanes_of(q)], out_sem.at[0, q])

    def gp_copy(q):
        lanes = lanes_of(q)
        return pltpu.make_async_copy(gs.at[:, lanes], gp_hbm.at[:, lanes], out_sem.at[1, q])

    def enter_forward(p, carry):
        r, k, q = order_in(p)

        @pl.when(r > 0)
        def _():
            f2(r, k).wait_recv()

        start = inf[q]
        base = start.astype(F32)
        total = None
        for b in range(NB):
            if b > 0:
                tot_b = tot[q, pl.ds(b - 1, 1), :]
                total = tot_b if b == 1 else total + tot_b
                start = (ls[q, b - 1] + jnp.exp(total) * base).astype(BF)
            carried = growth[q, blk(b), :] * dot(act_c[blk(b), :], start)
            sx[q, blk(b), :] = (acc_o[q, blk(b), :] + carried).astype(BF)
            grad_c[blk(b), :] += dot_nt(gw[q, blk(b), :], start)
        out_copy(q).start()
        return carry

    lax.fori_loop(0, NQ, enter_forward, 0)

    tail = pl.ds(T, HALO)

    def ghalo(src, dst, slot):
        return remote(src, dst, ghalo_s.at[slot], ghalo_r.at[slot], prv)

    def ghalo_x(q):
        return ghalo(gs.at[head, lanes_of(q)], gh.at[q], q)

    def ghalo_b():
        return ghalo(gpb.at[head], gpb.at[tail], NQ)

    def ghalo_c():
        return ghalo(gpc.at[head], gpc.at[tail], NQ + 1)

    def send_halo(copy):
        @pl.when(me > 0)
        def _():
            copy.start()

    def take_halo(copy, dst):
        @pl.when(me < 15)
        def _():
            copy.wait_recv()

        @pl.when(me == 15)
        def _():
            dst[...] = jnp.zeros((HALO, W), BF)

    def enter_backward(p, carry):
        r, k, q = order_in(p)

        @pl.when(r > 0)
        def _():
            b2(r, k).wait_recv()

        after = inb[q]
        base = after.astype(F32)
        total = None
        for b in reversed(range(NB)):
            if b < NB - 1:
                tot_b = tot[q, pl.ds(b + 1, 1), :]
                total = tot_b if b == NB - 2 else total + tot_b
                after = (la[q, b] + jnp.exp(total) * base).astype(BF)
            outer = stte[q, blk(b), :] * dot(act_b[blk(b), :], after)
            grads = (acc_g[q, blk(b), :] + outer) * slope[q, blk(b), :]
            gs[blk(b), lanes_of(q)] = grads.astype(BF)
            grad_b[blk(b), :] += dot_nt(wx[q, blk(b), :], after)
        send_halo(ghalo_x(q))
        gp_copy(q).start()
        return carry

    for b in range(NB):
        pair_sum = ps[b] * lower_f
        pair_t = jnp.transpose(pair_sum).astype(BF)
        grad_b[blk(b), :] = dot(pair_t, act_c[blk(b), :])
        into_c = grad_c[blk(b), :] + dot(pair_sum.astype(BF), act_b[blk(b), :])
        gpc[blk(b), :] = (into_c * slope_c[blk(b), :]).astype(BF)
    send_halo(ghalo_c())
    gpc_out[pl.ds(0, T), :] = gpc[pl.ds(0, T), :]

    lax.fori_loop(0, NQ, enter_backward, 0)

    for b in range(NB):
        gpb[blk(b), :] = (grad_b[blk(b), :] * slope_b[blk(b), :]).astype(BF)
    send_halo(ghalo_b())
    gpb_out[pl.ds(0, T), :] = gpb[pl.ds(0, T), :]
    for q in range(NQ):
        take_halo(ghalo_x(q), gh.at[q])
        gh_out[:, q * W : (q + 1) * W] = gh[q]
    for ref, out, copy in ((gpb, gpb_out, ghalo_b()), (gpc, gpc_out, ghalo_c())):
        take_halo(copy, ref.at[tail])
        out[tail, :] = ref[tail, :]

    for q in range(NQ):
        out_copy(q).wait()
        gp_copy(q).wait()

    @pl.when(me < 15)
    def _():
        for h in halos:
            h.wait_send()

    @pl.when(me > 0)
    def _():
        for q in range(NQ):
            ghalo_x(q).wait_send()
        ghalo_b().wait_send()
        ghalo_c().wait_send()

    for k in range(2):
        for r in range(1, 4):
            f1(r, k).wait_send()
            b1(r, k).wait_send()
            f2(r, k).wait_send()
            b2(r, k).wait_send()

            @pl.when(y + r <= 3)
            def _():
                yf_cp(r, k).wait_send()

            @pl.when(y - (4 - r) >= 0)
            def _():
                yb_cp(r, k).wait_send()


def back_kernel(
    out_hbm, gp_hbm, gh_hbm, gpb, gpc, kx, kb, kc, out_ref, gx_ref, gb_ref, gc_ref,
    out_v, gp_v, gx_v, in_sem, out_sem,
):
    def rows(i):
        return pl.ds(i * BLOCK, BLOCK)

    loads = [pltpu.make_async_copy(gh_hbm, gp_v.at[pl.ds(T, HALO)], in_sem.at[2 * NB])]
    for i in reversed(range(NB)):
        loads.append(pltpu.make_async_copy(gp_hbm.at[rows(i)], gp_v.at[rows(i)], in_sem.at[i]))
    passed = [
        pltpu.make_async_copy(out_hbm.at[rows(i)], out_v.at[rows(i)], in_sem.at[NB + i])
        for i in range(NB)
    ]
    for copy in loads + passed:
        copy.start()

    def back(value, taps, count):
        value = value.astype(F32)
        size = value.shape[0]
        grad = taps[3:4] * value[:count]
        for k in range(3):
            grad = grad + taps[k : k + 1] * pltpu.roll(value, size - (3 - k), 0)[:count]
        return grad.astype(BF)

    gb_ref[...] = back(gpb[...], kb[...], T)
    gc_ref[...] = back(gpc[...], kc[...], T)
    stores = []
    loads[0].wait()
    for i in reversed(range(NB)):
        loads[NB - i].wait()

        def slab(q, carry):
            lanes = pl.ds(pl.multiple_of(q * W, W), W)
            value = gp_v[pl.ds(i * BLOCK, BLOCK + HALO), lanes]
            gx_v[rows(i), lanes] = back(value, kx[:, lanes], BLOCK)
            return carry

        lax.fori_loop(0, NQ, slab, 0)
        stores.append(pltpu.make_async_copy(gx_v.at[rows(i)], gx_ref.at[rows(i)], out_sem.at[i]))
        stores[-1].start()
    for i in range(NB):
        passed[i].wait()
        stores.append(
            pltpu.make_async_copy(out_v.at[rows(i)], out_ref.at[rows(i)], out_sem.at[NB + i])
        )
        stores[-1].start()
    for copy in stores:
        copy.wait()


def on_device(x, b, c, kx, kb, kc, step, dlog, skip, g):
    hbm = pl.BlockSpec(memory_space=pl.ANY)
    vmem = pl.BlockSpec(memory_space=pltpu.VMEM)
    dma = pltpu.SemaphoreType.DMA
    full = (NQ, T, W)
    scratch = [
        pltpu.VMEM((T + HALO, NQ * W), BF),
        pltpu.VMEM((T + HALO, ST), BF),
        pltpu.VMEM((T + HALO, ST), BF),
        pltpu.VMEM((T, NQ * W), BF),
        pltpu.VMEM((T + 16, 6 * H), BF),
        pltpu.VMEM((NQ, 8, T), F32),
        pltpu.VMEM((T + 16, 2 * W), F32),
        pltpu.VMEM((NQ, 8, W), F32),
        pltpu.VMEM((NQ, 8, W), F32),
        pltpu.VMEM(full, F32),
        pltpu.VMEM(full, F32),
        pltpu.VMEM(full, F32),
        pltpu.VMEM(full, F32),
        pltpu.VMEM(full, F32),
        pltpu.VMEM(full, BF),
        pltpu.VMEM(full, BF),
        pltpu.VMEM(full, BF),
        pltpu.VMEM((NQ, 3, ST, W), F32),
        pltpu.VMEM((NQ, 3, ST, W), F32),
        pltpu.VMEM((NQ, HALO, W), BF),
        pltpu.VMEM((T + HALO, ST), BF),
        pltpu.VMEM((T + HALO, ST), BF),
        pltpu.VMEM((T, ST), BF),
        pltpu.VMEM((T, ST), BF),
        pltpu.VMEM((NB, ST, BLOCK), BF),
        pltpu.VMEM((NB, ST, BLOCK), BF),
        pltpu.VMEM((T, ST), F32),
        pltpu.VMEM((T, ST), F32),
        pltpu.VMEM((NB, BLOCK, BLOCK), F32),
        pltpu.VMEM((NB, BLOCK, BLOCK), F32),
        pltpu.VMEM((NB, BLOCK, BLOCK), F32),
        pltpu.VMEM((T, ST), F32),
        pltpu.VMEM((T, ST), F32),
        pltpu.VMEM((NQ, LROWS, W), BF),
        pltpu.VMEM((NQ, ST, W), BF),
        pltpu.VMEM((NQ, LROWS, W), BF),
        pltpu.VMEM((NQ, ST, W), BF),
        pltpu.VMEM((2, LROWS, W), BF),
        pltpu.VMEM((2, LROWS, W), BF),
        pltpu.VMEM((NQ, LROWS, W), BF),
        pltpu.VMEM((NQ, LROWS, W), BF),
        pltpu.VMEM((NQ, ST, W), BF),
        pltpu.VMEM((NQ, ST, W), BF),
        pltpu.VMEM((NQ, ST, W), BF),
        pltpu.VMEM((NQ, ST, W), BF),
        pltpu.VMEM((2, ST, W), F32),
        pltpu.VMEM((2, ST, W), F32),
        dma((4,)), dma((2, NQ)), dma((3,)), dma((3,)), dma((10,)), dma((10,)),
    ] + [dma((4, 2))] * 12
    out, gp, gh, gpb, gpc = pl.pallas_call(
        kernel,
        out_shape=(
            jax.ShapeDtypeStruct(x.shape, BF),
            jax.ShapeDtypeStruct(x.shape, BF),
            jax.ShapeDtypeStruct((HALO, NQ * W), BF),
            jax.ShapeDtypeStruct((T + HALO, ST), BF),
            jax.ShapeDtypeStruct((T + HALO, ST), BF),
        ),
        in_specs=[hbm] * 3 + [vmem] * 6 + [hbm],
        out_specs=(hbm, hbm, vmem, vmem, vmem),
        scratch_shapes=scratch,
        compiler_params=pltpu.CompilerParams(
            collective_id=0, has_side_effects=True, vmem_limit_bytes=67043328
        ),
    )(x, b, c, kx, kb, kc, step.T, dlog.reshape(1, H), skip.reshape(1, H), g)
    return pl.pallas_call(
        back_kernel,
        out_shape=(
            jax.ShapeDtypeStruct(x.shape, BF),
            jax.ShapeDtypeStruct(x.shape, BF),
            jax.ShapeDtypeStruct(b.shape, BF),
            jax.ShapeDtypeStruct(c.shape, BF),
        ),
        in_specs=[hbm] * 3 + [vmem] * 5,
        out_specs=(hbm, hbm, vmem, vmem),
        scratch_shapes=[
            pltpu.VMEM((T, NQ * W), BF),
            pltpu.VMEM((T + HALO, NQ * W), BF),
            pltpu.VMEM((T, NQ * W), BF),
            dma((2 * NB + 1,)),
            dma((2 * NB,)),
        ],
    )(out, gp, gh, gpb, gpc, kx, kb, kc)


def solution(mesh):
    rows = P(("doc", "context"), "head")
    taps = P(None, "head")
    return jax.shard_map(
        on_device,
        mesh=mesh,
        in_specs=(rows, rows, rows, taps, taps, taps, rows, P("head"), P("head"), rows),
        out_specs=(rows, rows, rows, rows),
        check_vma=False,
    )
```

```python
import jax
import jax.numpy as jnp
from jax import lax
from jax.experimental import pallas as pl
from jax.experimental.pallas import tpu as pltpu
from jax.sharding import PartitionSpec as P

BLOCK = 128
NB = 4
T = 512
H = 32
W = 256
NQ = 8
ST = 256
HALO = 16
LROWS = ST + HALO
MESH = pl.DeviceIdType.MESH
F32 = jnp.float32
BF = jnp.bfloat16


def dot(a, b):
    return jnp.dot(a, b, preferred_element_type=F32)


def dot_nt(a, b):
    return lax.dot_general(a, b, (((1,), (1,)), ((), ())), preferred_element_type=F32)


def split3(v):
    hi = v.astype(BF)
    rest = v - hi.astype(F32)
    mid = rest.astype(BF)
    low = (rest - mid.astype(F32)).astype(BF)
    return hi, mid, low


def sigmoid(v):
    return 1.0 / (1.0 + jnp.exp(-v))


def tail_rows(row):
    hi, mid, low = split3(row)
    index = lax.broadcasted_iota(jnp.int32, (HALO, row.shape[1]), 0)
    zero = jnp.zeros((HALO, row.shape[1]), F32)
    full = jnp.where(
        index == 0,
        hi.astype(F32),
        jnp.where(index == 1, mid.astype(F32), jnp.where(index == 2, low.astype(F32), zero)),
    )
    return full.astype(BF)


def tail_sum(rows):
    return jnp.sum(rows.astype(F32), axis=0, keepdims=True)


def kernel(
    x_hbm, b_hbm, c_hbm, kx, kb, kc, step, dlog, skip, g_hbm,
    out_hbm, gp_hbm, gh_out, gpb_out, gpc_out,
    xp, bp, cp, gs, lh, cumt, ex, tot, ske,
    slope, growth, stte, acc_o, acc_g, sx, wx, gw, ls, la,
    gh, gpb, gpc, act_b, act_c, bt, ct, slope_b, slope_c,
    ps, sl, su, grad_b, grad_c,
    sf, sb, rf, rb, tf, tb, yf, yb, of, ob, inf, inb, rs_f, rs_b,
    in_sem, out_sem, halo_s, halo_r, ghalo_s, ghalo_r,
    f1s, f1r, b1s, b1r, yfs, yfr, ybs, ybr, f2s, f2r, b2s, b2r,
):
    me = lax.axis_index("context")
    y = me // 4
    x = me % 4
    nxt = (me + 1) % 16
    prv = (me + 15) % 16

    def remote(src, dst, s, r, peer):
        return pltpu.make_async_remote_copy(
            src_ref=src, dst_ref=dst, send_sem=s, recv_sem=r,
            device_id={"context": peer}, device_id_type=MESH,
        )

    barrier = pltpu.get_barrier_semaphore()
    peers = [nxt, prv]
    peers += [y * 4 + (x + r) % 4 for r in range(1, 4)]
    peers += [((y + r) % 4) * 4 + x for r in range(1, 4)]
    for peer in peers:
        pl.semaphore_signal(barrier, inc=1, device_id={"context": peer}, device_id_type=MESH)

    body = pl.ds(HALO, T)
    loads = [
        pltpu.make_async_copy(b_hbm, bp.at[body], in_sem.at[0]),
        pltpu.make_async_copy(c_hbm, cp.at[body], in_sem.at[1]),
        pltpu.make_async_copy(x_hbm, xp.at[body], in_sem.at[2]),
        pltpu.make_async_copy(g_hbm, gs, in_sem.at[3]),
    ]
    for load in loads:
        load.start()

    rate = -jnp.exp(jnp.transpose(jnp.broadcast_to(dlog[...], (8, H)))[:, 0:1])
    lower = (
        lax.broadcasted_iota(jnp.int32, (BLOCK, BLOCK), 0)
        >= lax.broadcasted_iota(jnp.int32, (BLOCK, BLOCK), 1)
    )
    lower_f = lower.astype(F32)
    upper_f = (
        lax.broadcasted_iota(jnp.int32, (BLOCK, BLOCK), 0)
        <= lax.broadcasted_iota(jnp.int32, (BLOCK, BLOCK), 1)
    ).astype(F32)
    upper_b = upper_f.astype(BF)
    for b in range(NB):
        rows = pl.ds(b * BLOCK, BLOCK)
        step_b = step[:, rows]
        logs = split3(step_b * rate)
        flipped = dot(logs[0], upper_b) + dot(logs[1], upper_b) + dot(logs[2], upper_b)
        for q in range(NQ):
            cumt[q, 0:4, rows] = flipped[4 * q : 4 * q + 4]
        pieces = split3(jnp.transpose(flipped)) + split3(jnp.transpose(step_b))
        lh[rows, :] = jnp.concatenate([p.astype(F32) for p in pieces], axis=1).astype(BF)
    skips = split3(jnp.broadcast_to(skip[...], (16, H)))
    zero_s = jnp.zeros((16, 3 * H), F32)
    lh[pl.ds(T, 16), :] = jnp.concatenate(
        [p.astype(F32) for p in skips] + [zero_s], axis=1
    ).astype(BF)
    ps[...] = jnp.zeros_like(ps)
    grad_c[...] = jnp.zeros_like(grad_c)

    pl.semaphore_wait(barrier, 8)

    head = pl.ds(0, HALO)
    last = pl.ds(T - HALO, HALO)
    halos = [
        remote(b_hbm.at[last], bp.at[head], halo_s.at[0], halo_r.at[0], nxt),
        remote(c_hbm.at[last], cp.at[head], halo_s.at[1], halo_r.at[1], nxt),
        remote(x_hbm.at[last], xp.at[head], halo_s.at[2], halo_r.at[2], nxt),
    ]

    @pl.when(me < 15)
    def _():
        for h in halos:
            h.start()

    @pl.when(me == 0)
    def _():
        for ref in (bp, cp, xp):
            ref[head, :] = jnp.zeros((HALO, ref.shape[1]), BF)

    def blk(b):
        return pl.ds(b * BLOCK, BLOCK)

    def lanes_of(q):
        return pl.ds(pl.multiple_of(q * W, W), W)

    def spread(q, carry):
        depth = lax.broadcasted_iota(jnp.int32, (6 * H, 2 * W), 0)
        col = lax.broadcasted_iota(jnp.int32, (6 * H, 2 * W), 1)
        hit = (depth % H == 4 * q + (col % W) // 64) & ((depth // (3 * H)) == (col // W))
        ex[...] = dot(lh[...], hit.astype(F32).astype(BF))
        ske[q] = ex[pl.ds(T, 8), 0:W]
        for b in range(NB):
            cum = ex[blk(b), 0:W]
            steps = ex[blk(b), W : 2 * W]
            tot_b = ex[pl.ds(b * BLOCK + BLOCK - 1, 1), 0:W]
            tot[q, pl.ds(b, 1), :] = tot_b
            to_end = jnp.exp(tot_b - cum)
            growth[q, blk(b), :] = jnp.exp(cum)
            acc_o[q, blk(b), :] = to_end
            acc_g[q, blk(b), :] = steps
            stte[q, blk(b), :] = steps * to_end
        return carry

    lax.fori_loop(0, NQ, spread, 0)

    for load in loads:
        load.wait()

    @pl.when(me > 0)
    def _():
        for h in halos:
            h.wait_recv()

    def conv(ref, lanes, taps):
        padded = ref[:, lanes].astype(F32)
        pre = taps[3:4] * padded[HALO:]
        for k in range(3):
            pre = pre + taps[k : k + 1] * pltpu.roll(padded, 3 - k, 0)[HALO:]
        return pre

    def prepare(ref, taps, act, act_t, slo):
        pre = conv(ref, pl.ds(0, ST), taps[...])
        sig = sigmoid(pre)
        slo[...] = sig * (1.0 + pre * (1.0 - sig))
        value = (pre * sig).astype(BF)
        act[...] = value
        for b in range(NB):
            act_t[b] = jnp.transpose(value[b * BLOCK : (b + 1) * BLOCK].astype(F32)).astype(BF)

    prepare(bp, kb, act_b, bt, slope_b)

    def order(p):
        far = p < 6
        r = jnp.where(far, p % 3 + 1, 0)
        k = jnp.where(far, p // 3, p - 6)
        return r, k, ((x + r) % 4) * 2 + k

    def row_peer(r):
        return y * 4 + (x + r) % 4

    def f1(r, k):
        return remote(
            sf.at[((x + r) % 4) * 2 + k], rf.at[x * 2 + k], f1s.at[r, k], f1r.at[r, k], row_peer(r)
        )

    def b1(r, k):
        return remote(
            sb.at[((x + r) % 4) * 2 + k], rb.at[x * 2 + k], b1s.at[r, k], b1r.at[r, k], row_peer(r)
        )

    def f2(r, k):
        return remote(
            of.at[((x + r) % 4) * 2 + k], inf.at[x * 2 + k], f2s.at[r, k], f2r.at[r, k], row_peer(r)
        )

    def b2(r, k):
        return remote(
            ob.at[((x + r) % 4) * 2 + k], inb.at[x * 2 + k], b2s.at[r, k], b2r.at[r, k], row_peer(r)
        )

    def yf_cp(r, k):
        return remote(
            tf.at[k], yf.at[y * 2 + k], yfs.at[r, k], yfr.at[y, k], ((y + r) % 4) * 4 + x
        )

    def yb_cp(r, k):
        return remote(
            tb.at[k], yb.at[y * 2 + k], ybs.at[r, k], ybr.at[y, k], ((y + r) % 4) * 4 + x
        )

    def forward_local(p, carry):
        r, k, q = order(p)
        lanes = lanes_of(q)
        pre = conv(xp, lanes, kx[:, lanes])
        slope[q] = pre
        act = (pre * sigmoid(pre)).astype(BF).astype(F32)
        scaled = (act * acc_g[q]).astype(BF)
        sx[q] = scaled
        weighted = (scaled.astype(F32) * acc_o[q]).astype(BF)
        wx[q] = weighted
        state = None
        total = None
        for b in range(NB):
            tot_b = tot[q, pl.ds(b, 1), :]
            grown = dot(bt[b], weighted[b * BLOCK : (b + 1) * BLOCK])
            if b == 0:
                state, total = grown, tot_b
            else:
                ls[q, b - 1] = state
                state = jnp.exp(tot_b) * state + grown
                total = total + tot_b
        state = state.astype(BF)
        tail = tail_rows(total)

        @pl.when(r == 0)
        def _():
            rf[q, 0:ST, :] = state
            rf[q, ST:LROWS, :] = tail

        @pl.when(r > 0)
        def _():
            sf[q, 0:ST, :] = state
            sf[q, ST:LROWS, :] = tail
            f1(r, k).start()

        return carry

    lax.fori_loop(0, NQ, forward_local, 0)

    prepare(cp, kc, act_c, ct, slope_c)

    def backward_local(p, carry):
        r, k, q = order(p)
        lanes = lanes_of(q)
        state = None
        for b in reversed(range(NB)):
            grads = (gs[blk(b), lanes].astype(F32) * growth[q, blk(b), :]).astype(BF)
            gw[q, blk(b), :] = grads
            grown = dot(ct[b], grads)
            if b == NB - 1:
                state = grown
            else:
                la[q, b] = state
                state = jnp.exp(tot[q, pl.ds(b, 1), :]) * state + grown
        state = state.astype(BF)

        @pl.when(r == 0)
        def _():
            rb[q] = state

        @pl.when(r > 0)
        def _():
            sb[q] = state
            b1(r, k).start()

        return carry

    lax.fori_loop(0, NQ, backward_local, 0)

    for b in range(NB):
        scores = dot_nt(act_c[blk(b), :], act_b[blk(b), :])
        sl[b] = scores * lower_f
        su[b] = jnp.transpose(scores) * upper_f

    left = lax.broadcasted_iota(jnp.int32, (BLOCK, BLOCK), 1) < 64

    def halves(value):
        zero = jnp.zeros_like(value)
        return jnp.concatenate([jnp.where(left, value, zero), jnp.where(left, zero, value)], axis=0)

    def intra(q, carry):
        depth = lax.broadcasted_iota(jnp.int32, (6 * H, 2 * W), 0)
        col = lax.broadcasted_iota(jnp.int32, (6 * H, 2 * W), 1)
        hit = (depth % H == 4 * q + col // BLOCK) & (depth < 3 * H)
        hit = hit.astype(F32).astype(BF)
        for b in range(NB):
            down = dot(lh[blk(b), :], hit)
            for pair in range(2):
                part = pl.ds(pair * BLOCK, BLOCK)
                across = jnp.concatenate(
                    [cumt[q, pl.ds(2 * pair + i, 1), blk(b)] for i in range(2)], axis=1
                )
                differ = down[:, pair * W : (pair + 1) * W] - across
                table = jnp.exp(-jnp.abs(differ))
                scores = jnp.concatenate([sl[b], sl[b]], axis=1)
                scores_t = jnp.concatenate([su[b], su[b]], axis=1)
                mixing = (table * scores).astype(BF)
                mixing_t = (table * scores_t).astype(BF)
                scaled = sx[q, blk(b), part]
                grads = gs[blk(b), pl.ds(pl.multiple_of(q * W + pair * BLOCK, BLOCK), BLOCK)]
                wide_x = halves(scaled)
                pre = slope[q, blk(b), part]
                sig = sigmoid(pre)
                slope[q, blk(b), part] = sig * (1.0 + pre * (1.0 - sig))
                direct = ske[q, 0:1, part] * (pre * sig).astype(BF).astype(F32)
                acc_o[q, blk(b), part] = direct + dot(mixing, wide_x)
                inner = dot(mixing_t, halves(grads))
                acc_g[q, blk(b), part] = (
                    acc_g[q, blk(b), part] * inner + ske[q, 0:1, part] * grads.astype(F32)
                )
                both = table * dot_nt(grads, wide_x)
                ps[b] += both[:, :BLOCK] + both[:, BLOCK:]
        return carry

    def row_forward(k):
        state, total = None, None
        for i in range(4):
            local = rf[i * 2 + k, 0:ST, :].astype(F32)
            own = tail_sum(rf[i * 2 + k, ST:LROWS, :])
            if i == 0:
                state, total = local, own
            else:
                state = jnp.exp(own) * state + local
                total = total + own
        tf[k, 0:ST, :] = state.astype(BF)
        tf[k, ST:LROWS, :] = tail_rows(total)
        rs_f[k] = jnp.zeros((ST, W), F32)
        for r in range(1, 4):
            @pl.when(y + r <= 3)
            def _():
                yf_cp(r, k).start()

    def row_backward(k):
        state = None
        for i in reversed(range(4)):
            local = rb[i * 2 + k].astype(F32)
            own = tail_sum(rf[i * 2 + k, ST:LROWS, :])
            state = local if i == 3 else jnp.exp(own) * state + local
        tb[k, 0:ST, :] = state.astype(BF)
        tb[k, ST:LROWS, :] = tf[k, ST:LROWS, :]
        rs_b[k] = jnp.zeros((ST, W), F32)
        for r in range(1, 4):
            @pl.when(y - (4 - r) >= 0)
            def _():
                yb_cp(r, k).start()

    def finish_forward(k):
        for i in range(3):
            @pl.when(i < y)
            def _():
                remote(
                    tf.at[k], yf.at[i * 2 + k], yfs.at[1, k], yfr.at[i, k], nxt
                ).wait_recv()
                own = tail_sum(yf[i * 2 + k, ST:LROWS, :])
                rs_f[k] = jnp.exp(own) * rs_f[k] + yf[i * 2 + k, 0:ST, :].astype(F32)
        state = rs_f[k]
        for i in range(4):
            out = state.astype(BF)
            of[i * 2 + k] = out

            @pl.when(x == i)
            def _():
                inf[i * 2 + k] = out

            if i < 3:
                own = tail_sum(rf[i * 2 + k, ST:LROWS, :])
                state = jnp.exp(own) * state + rf[i * 2 + k, 0:ST, :].astype(F32)
        for r in range(1, 4):
            f2(r, k).start()

    def finish_backward(k):
        for i in reversed(range(1, 4)):
            @pl.when(i > y)
            def _():
                remote(
                    tb.at[k], yb.at[i * 2 + k], ybs.at[1, k], ybr.at[i, k], nxt
                ).wait_recv()
                own = tail_sum(yb[i * 2 + k, ST:LROWS, :])
                rs_b[k] = jnp.exp(own) * rs_b[k] + yb[i * 2 + k, 0:ST, :].astype(F32)
        state = rs_b[k]
        for i in reversed(range(4)):
            out = state.astype(BF)
            ob[i * 2 + k] = out

            @pl.when(x == i)
            def _():
                inb[i * 2 + k] = out

            if i > 0:
                own = tail_sum(rf[i * 2 + k, ST:LROWS, :])
                state = jnp.exp(own) * state + rb[i * 2 + k].astype(F32)
        for r in range(1, 4):
            b2(r, k).start()

    def take_forward(k):
        for r in range(1, 4):
            f1(r, k).wait_recv()
        row_forward(k)

    def take_backward(k):
        for r in range(1, 4):
            b1(r, k).wait_recv()
        row_backward(k)

    def order_in(p):
        r = p % 4
        k = p // 4
        return r, k, ((x + 4 - r) % 4) * 2 + k

    def out_copy(q):
        return pltpu.make_async_copy(sx.at[q], out_hbm.at[:, lanes_of(q)], out_sem.at[0, q])

    def gp_copy(q):
        lanes = lanes_of(q)
        return pltpu.make_async_copy(gs.at[:, lanes], gp_hbm.at[:, lanes], out_sem.at[1, q])

    def enter_forward(p, carry):
        r, k, q = order_in(p)

        @pl.when(r > 0)
        def _():
            f2(r, k).wait_recv()

        start = inf[q]
        base = start.astype(F32)
        total = None
        for b in range(NB):
            if b > 0:
                tot_b = tot[q, pl.ds(b - 1, 1), :]
                total = tot_b if b == 1 else total + tot_b
                start = (ls[q, b - 1] + jnp.exp(total) * base).astype(BF)
            carried = growth[q, blk(b), :] * dot(act_c[blk(b), :], start)
            sx[q, blk(b), :] = (acc_o[q, blk(b), :] + carried).astype(BF)
            grad_c[blk(b), :] += dot_nt(gw[q, blk(b), :], start)
        out_copy(q).start()
        return carry

    take_forward(0)
    lax.fori_loop(0, 3, intra, 0)
    take_forward(1)
    lax.fori_loop(3, 6, intra, 0)
    finish_forward(0)
    take_backward(0)
    lax.fori_loop(6, 7, intra, 0)
    finish_forward(1)
    take_backward(1)
    lax.fori_loop(7, NQ, intra, 0)
    finish_backward(0)
    lax.fori_loop(0, 4, enter_forward, 0)
    finish_backward(1)
    lax.fori_loop(4, NQ, enter_forward, 0)

    tail = pl.ds(T, HALO)

    def ghalo(src, dst, slot):
        return remote(src, dst, ghalo_s.at[slot], ghalo_r.at[slot], prv)

    def ghalo_x(q):
        return ghalo(gs.at[head, lanes_of(q)], gh.at[q], q)

    def ghalo_b():
        return ghalo(gpb.at[head], gpb.at[tail], NQ)

    def ghalo_c():
        return ghalo(gpc.at[head], gpc.at[tail], NQ + 1)

    def send_halo(copy):
        @pl.when(me > 0)
        def _():
            copy.start()

    def take_halo(copy, dst):
        @pl.when(me < 15)
        def _():
            copy.wait_recv()

        @pl.when(me == 15)
        def _():
            dst[...] = jnp.zeros((HALO, W), BF)

    def enter_backward(p, carry):
        r, k, q = order_in(p)

        @pl.when(r > 0)
        def _():
            b2(r, k).wait_recv()

        after = inb[q]
        base = after.astype(F32)
        total = None
        for b in reversed(range(NB)):
            if b < NB - 1:
                tot_b = tot[q, pl.ds(b + 1, 1), :]
                total = tot_b if b == NB - 2 else total + tot_b
                after = (la[q, b] + jnp.exp(total) * base).astype(BF)
            outer = stte[q, blk(b), :] * dot(act_b[blk(b), :], after)
            grads = (acc_g[q, blk(b), :] + outer) * slope[q, blk(b), :]
            gs[blk(b), lanes_of(q)] = grads.astype(BF)
            grad_b[blk(b), :] += dot_nt(wx[q, blk(b), :], after)
        send_halo(ghalo_x(q))
        gp_copy(q).start()
        return carry

    for b in range(NB):
        pair_sum = ps[b] * lower_f
        pair_t = jnp.transpose(pair_sum).astype(BF)
        grad_b[blk(b), :] = dot(pair_t, act_c[blk(b), :])
        into_c = grad_c[blk(b), :] + dot(pair_sum.astype(BF), act_b[blk(b), :])
        gpc[blk(b), :] = (into_c * slope_c[blk(b), :]).astype(BF)
    send_halo(ghalo_c())
    gpc_out[pl.ds(0, T), :] = gpc[pl.ds(0, T), :]

    lax.fori_loop(0, NQ, enter_backward, 0)

    for b in range(NB):
        gpb[blk(b), :] = (grad_b[blk(b), :] * slope_b[blk(b), :]).astype(BF)
    send_halo(ghalo_b())
    gpb_out[pl.ds(0, T), :] = gpb[pl.ds(0, T), :]
    for q in range(NQ):
        take_halo(ghalo_x(q), gh.at[q])
        gh_out[:, q * W : (q + 1) * W] = gh[q]
    for ref, out, copy in ((gpb, gpb_out, ghalo_b()), (gpc, gpc_out, ghalo_c())):
        take_halo(copy, ref.at[tail])
        out[tail, :] = ref[tail, :]

    for q in range(NQ):
        out_copy(q).wait()
        gp_copy(q).wait()

    @pl.when(me < 15)
    def _():
        for h in halos:
            h.wait_send()

    @pl.when(me > 0)
    def _():
        for q in range(NQ):
            ghalo_x(q).wait_send()
        ghalo_b().wait_send()
        ghalo_c().wait_send()

    for k in range(2):
        for r in range(1, 4):
            f1(r, k).wait_send()
            b1(r, k).wait_send()
            f2(r, k).wait_send()
            b2(r, k).wait_send()

            @pl.when(y + r <= 3)
            def _():
                yf_cp(r, k).wait_send()

            @pl.when(y - (4 - r) >= 0)
            def _():
                yb_cp(r, k).wait_send()


def back_kernel(
    out_hbm, gp_hbm, gh_hbm, gpb, gpc, kx, kb, kc, out_ref, gx_ref, gb_ref, gc_ref,
    out_v, gp_v, gx_v, in_sem, out_sem,
):
    def rows(i):
        return pl.ds(i * BLOCK, BLOCK)

    loads = [pltpu.make_async_copy(gh_hbm, gp_v.at[pl.ds(T, HALO)], in_sem.at[2 * NB])]
    for i in reversed(range(NB)):
        loads.append(pltpu.make_async_copy(gp_hbm.at[rows(i)], gp_v.at[rows(i)], in_sem.at[i]))
    passed = [
        pltpu.make_async_copy(out_hbm.at[rows(i)], out_v.at[rows(i)], in_sem.at[NB + i])
        for i in range(NB)
    ]
    for copy in loads + passed:
        copy.start()

    def back(value, taps, count):
        value = value.astype(F32)
        size = value.shape[0]
        grad = taps[3:4] * value[:count]
        for k in range(3):
            grad = grad + taps[k : k + 1] * pltpu.roll(value, size - (3 - k), 0)[:count]
        return grad.astype(BF)

    gb_ref[...] = back(gpb[...], kb[...], T)
    gc_ref[...] = back(gpc[...], kc[...], T)
    stores = []
    loads[0].wait()
    for i in reversed(range(NB)):
        loads[NB - i].wait()

        def slab(q, carry):
            lanes = pl.ds(pl.multiple_of(q * W, W), W)
            value = gp_v[pl.ds(i * BLOCK, BLOCK + HALO), lanes]
            gx_v[rows(i), lanes] = back(value, kx[:, lanes], BLOCK)
            return carry

        lax.fori_loop(0, NQ, slab, 0)
        stores.append(pltpu.make_async_copy(gx_v.at[rows(i)], gx_ref.at[rows(i)], out_sem.at[i]))
        stores[-1].start()
    for i in range(NB):
        passed[i].wait()
        stores.append(
            pltpu.make_async_copy(out_v.at[rows(i)], out_ref.at[rows(i)], out_sem.at[NB + i])
        )
        stores[-1].start()
    for copy in stores:
        copy.wait()


def on_device(x, b, c, kx, kb, kc, step, dlog, skip, g):
    hbm = pl.BlockSpec(memory_space=pl.ANY)
    vmem = pl.BlockSpec(memory_space=pltpu.VMEM)
    dma = pltpu.SemaphoreType.DMA
    full = (NQ, T, W)
    scratch = [
        pltpu.VMEM((T + HALO, NQ * W), BF),
        pltpu.VMEM((T + HALO, ST), BF),
        pltpu.VMEM((T + HALO, ST), BF),
        pltpu.VMEM((T, NQ * W), BF),
        pltpu.VMEM((T + 16, 6 * H), BF),
        pltpu.VMEM((NQ, 8, T), F32),
        pltpu.VMEM((T + 16, 2 * W), F32),
        pltpu.VMEM((NQ, 8, W), F32),
        pltpu.VMEM((NQ, 8, W), F32),
        pltpu.VMEM(full, F32),
        pltpu.VMEM(full, F32),
        pltpu.VMEM(full, F32),
        pltpu.VMEM(full, F32),
        pltpu.VMEM(full, F32),
        pltpu.VMEM(full, BF),
        pltpu.VMEM(full, BF),
        pltpu.VMEM(full, BF),
        pltpu.VMEM((NQ, 3, ST, W), F32),
        pltpu.VMEM((NQ, 3, ST, W), F32),
        pltpu.VMEM((NQ, HALO, W), BF),
        pltpu.VMEM((T + HALO, ST), BF),
        pltpu.VMEM((T + HALO, ST), BF),
        pltpu.VMEM((T, ST), BF),
        pltpu.VMEM((T, ST), BF),
        pltpu.VMEM((NB, ST, BLOCK), BF),
        pltpu.VMEM((NB, ST, BLOCK), BF),
        pltpu.VMEM((T, ST), F32),
        pltpu.VMEM((T, ST), F32),
        pltpu.VMEM((NB, BLOCK, BLOCK), F32),
        pltpu.VMEM((NB, BLOCK, BLOCK), F32),
        pltpu.VMEM((NB, BLOCK, BLOCK), F32),
        pltpu.VMEM((T, ST), F32),
        pltpu.VMEM((T, ST), F32),
        pltpu.VMEM((NQ, LROWS, W), BF),
        pltpu.VMEM((NQ, ST, W), BF),
        pltpu.VMEM((NQ, LROWS, W), BF),
        pltpu.VMEM((NQ, ST, W), BF),
        pltpu.VMEM((2, LROWS, W), BF),
        pltpu.VMEM((2, LROWS, W), BF),
        pltpu.VMEM((NQ, LROWS, W), BF),
        pltpu.VMEM((NQ, LROWS, W), BF),
        pltpu.VMEM((NQ, ST, W), BF),
        pltpu.VMEM((NQ, ST, W), BF),
        pltpu.VMEM((NQ, ST, W), BF),
        pltpu.VMEM((NQ, ST, W), BF),
        pltpu.VMEM((2, ST, W), F32),
        pltpu.VMEM((2, ST, W), F32),
        dma((4,)), dma((2, NQ)), dma((3,)), dma((3,)), dma((10,)), dma((10,)),
    ] + [dma((4, 2))] * 12
    out, gp, gh, gpb, gpc = pl.pallas_call(
        kernel,
        out_shape=(
            jax.ShapeDtypeStruct(x.shape, BF),
            jax.ShapeDtypeStruct(x.shape, BF),
            jax.ShapeDtypeStruct((HALO, NQ * W), BF),
            jax.ShapeDtypeStruct((T + HALO, ST), BF),
            jax.ShapeDtypeStruct((T + HALO, ST), BF),
        ),
        in_specs=[hbm] * 3 + [vmem] * 6 + [hbm],
        out_specs=(hbm, hbm, vmem, vmem, vmem),
        scratch_shapes=scratch,
        compiler_params=pltpu.CompilerParams(
            collective_id=0, has_side_effects=True, vmem_limit_bytes=67043328
        ),
    )(x, b, c, kx, kb, kc, step.T, dlog.reshape(1, H), skip.reshape(1, H), g)
    return pl.pallas_call(
        back_kernel,
        out_shape=(
            jax.ShapeDtypeStruct(x.shape, BF),
            jax.ShapeDtypeStruct(x.shape, BF),
            jax.ShapeDtypeStruct(b.shape, BF),
            jax.ShapeDtypeStruct(c.shape, BF),
        ),
        in_specs=[hbm] * 3 + [vmem] * 5,
        out_specs=(hbm, hbm, vmem, vmem),
        scratch_shapes=[
            pltpu.VMEM((T, NQ * W), BF),
            pltpu.VMEM((T + HALO, NQ * W), BF),
            pltpu.VMEM((T, NQ * W), BF),
            dma((2 * NB + 1,)),
            dma((2 * NB,)),
        ],
    )(out, gp, gh, gpb, gpc, kx, kb, kc)


def solution(mesh):
    rows = P(("doc", "context"), "head")
    taps = P(None, "head")
    return jax.shard_map(
        on_device,
        mesh=mesh,
        in_specs=(rows, rows, rows, taps, taps, taps, rows, P("head"), P("head"), rows),
        out_specs=(rows, rows, rows, rows),
        check_vma=False,
    )
```

```python
import jax
import jax.numpy as jnp
from jax import lax
from jax.experimental import pallas as pl
from jax.experimental.pallas import tpu as pltpu
from jax.sharding import PartitionSpec as P

BLOCK = 128
NB = 4
T = 512
H = 32
W = 256
NQ = 8
ST = 256
HALO = 16
LROWS = ST + HALO
MESH = pl.DeviceIdType.MESH
F32 = jnp.float32
BF = jnp.bfloat16


def dot(a, b):
    return jnp.dot(a, b, preferred_element_type=F32)


def dot_nt(a, b):
    return lax.dot_general(a, b, (((1,), (1,)), ((), ())), preferred_element_type=F32)


def split3(v):
    hi = v.astype(BF)
    rest = v - hi.astype(F32)
    mid = rest.astype(BF)
    low = (rest - mid.astype(F32)).astype(BF)
    return hi, mid, low


def sigmoid(v):
    return 1.0 / (1.0 + jnp.exp(-v))


def tail_rows(row):
    hi, mid, low = split3(row)
    index = lax.broadcasted_iota(jnp.int32, (HALO, row.shape[1]), 0)
    zero = jnp.zeros((HALO, row.shape[1]), F32)
    full = jnp.where(
        index == 0,
        hi.astype(F32),
        jnp.where(index == 1, mid.astype(F32), jnp.where(index == 2, low.astype(F32), zero)),
    )
    return full.astype(BF)


def tail_sum(rows):
    return jnp.sum(rows.astype(F32), axis=0, keepdims=True)


def kernel(
    x_hbm, b_hbm, c_hbm, kx, kb, kc, step, dlog, skip, g_hbm,
    out_hbm, gp_hbm, gh_out, gpb_out, gpc_out,
    xp, bp, cp, gs, lh, cumt, ex, tot, ske,
    slope, growth, stte, acc_o, acc_g, sx, wx, gw, ls, la,
    gh, gpb, gpc, act_b, act_c, bt, ct, slope_b, slope_c,
    ps, sl, su, grad_b, grad_c,
    sf, sb, rf, rb, tf, tb, yf, yb, of, ob, inf, inb, rs_f, rs_b,
    in_sem, out_sem, halo_s, halo_r, ghalo_s, ghalo_r,
    f1s, f1r, b1s, b1r, yfs, yfr, ybs, ybr, f2s, f2r, b2s, b2r,
):
    me = lax.axis_index("context")
    y = me // 4
    x = me % 4
    nxt = (me + 1) % 16
    prv = (me + 15) % 16

    def remote(src, dst, s, r, peer):
        return pltpu.make_async_remote_copy(
            src_ref=src, dst_ref=dst, send_sem=s, recv_sem=r,
            device_id={"context": peer}, device_id_type=MESH,
        )

    barrier = pltpu.get_barrier_semaphore()
    peers = [nxt, prv]
    peers += [y * 4 + (x + r) % 4 for r in range(1, 4)]
    peers += [((y + r) % 4) * 4 + x for r in range(1, 4)]
    for peer in peers:
        pl.semaphore_signal(barrier, inc=1, device_id={"context": peer}, device_id_type=MESH)

    body = pl.ds(HALO, T)
    loads = [
        pltpu.make_async_copy(b_hbm, bp.at[body], in_sem.at[0]),
        pltpu.make_async_copy(c_hbm, cp.at[body], in_sem.at[1]),
        pltpu.make_async_copy(x_hbm, xp.at[body], in_sem.at[2]),
        pltpu.make_async_copy(g_hbm, gs, in_sem.at[3]),
    ]
    for load in loads:
        load.start()

    rate = -jnp.exp(jnp.transpose(jnp.broadcast_to(dlog[...], (8, H)))[:, 0:1])
    lower = (
        lax.broadcasted_iota(jnp.int32, (BLOCK, BLOCK), 0)
        >= lax.broadcasted_iota(jnp.int32, (BLOCK, BLOCK), 1)
    )
    lower_f = lower.astype(F32)
    upper_f = (
        lax.broadcasted_iota(jnp.int32, (BLOCK, BLOCK), 0)
        <= lax.broadcasted_iota(jnp.int32, (BLOCK, BLOCK), 1)
    ).astype(F32)
    upper_b = upper_f.astype(BF)
    for b in range(NB):
        rows = pl.ds(b * BLOCK, BLOCK)
        step_b = step[:, rows]
        logs = split3(step_b * rate)
        flipped = dot(logs[0], upper_b) + dot(logs[1], upper_b) + dot(logs[2], upper_b)
        for q in range(NQ):
            cumt[q, 0:4, rows] = flipped[4 * q : 4 * q + 4]
        pieces = split3(jnp.transpose(flipped)) + split3(jnp.transpose(step_b))
        lh[rows, :] = jnp.concatenate([p.astype(F32) for p in pieces], axis=1).astype(BF)
    skips = split3(jnp.broadcast_to(skip[...], (16, H)))
    zero_s = jnp.zeros((16, 3 * H), F32)
    lh[pl.ds(T, 16), :] = jnp.concatenate(
        [p.astype(F32) for p in skips] + [zero_s], axis=1
    ).astype(BF)
    ps[...] = jnp.zeros_like(ps)
    grad_c[...] = jnp.zeros_like(grad_c)

    pl.semaphore_wait(barrier, 8)

    head = pl.ds(0, HALO)
    last = pl.ds(T - HALO, HALO)
    halos = [
        remote(b_hbm.at[last], bp.at[head], halo_s.at[0], halo_r.at[0], nxt),
        remote(c_hbm.at[last], cp.at[head], halo_s.at[1], halo_r.at[1], nxt),
        remote(x_hbm.at[last], xp.at[head], halo_s.at[2], halo_r.at[2], nxt),
    ]

    @pl.when(me < 15)
    def _():
        for h in halos:
            h.start()

    @pl.when(me == 0)
    def _():
        for ref in (bp, cp, xp):
            ref[head, :] = jnp.zeros((HALO, ref.shape[1]), BF)

    def blk(b):
        return pl.ds(b * BLOCK, BLOCK)

    def lanes_of(q):
        return pl.ds(pl.multiple_of(q * W, W), W)

    def order(p):
        far = p < 6
        r = jnp.where(far, jnp.where(p % 3 == 0, 2, jnp.where(p % 3 == 1, 1, 3)), 0)
        k = jnp.where(far, p // 3, p - 6)
        return r, k, ((x + r) % 4) * 2 + k

    def spread(p, carry):
        q = order(p)[2]
        depth = lax.broadcasted_iota(jnp.int32, (6 * H, 2 * W), 0)
        col = lax.broadcasted_iota(jnp.int32, (6 * H, 2 * W), 1)
        hit = (depth % H == 4 * q + (col % W) // 64) & ((depth // (3 * H)) == (col // W))
        ex[...] = dot(lh[...], hit.astype(F32).astype(BF))
        ske[q] = ex[pl.ds(T, 8), 0:W]
        for b in range(NB):
            cum = ex[blk(b), 0:W]
            steps = ex[blk(b), W : 2 * W]
            tot_b = ex[pl.ds(b * BLOCK + BLOCK - 1, 1), 0:W]
            tot[q, pl.ds(b, 1), :] = tot_b
            to_end = jnp.exp(tot_b - cum)
            growth[q, blk(b), :] = jnp.exp(cum)
            acc_o[q, blk(b), :] = to_end
            acc_g[q, blk(b), :] = steps
            stte[q, blk(b), :] = steps * to_end
        return carry

    lax.fori_loop(0, 3, spread, 0)

    for load in loads:
        load.wait()

    @pl.when(me > 0)
    def _():
        for h in halos:
            h.wait_recv()

    def conv(ref, lanes, taps):
        padded = ref[:, lanes].astype(F32)
        pre = taps[3:4] * padded[HALO:]
        for k in range(3):
            pre = pre + taps[k : k + 1] * pltpu.roll(padded, 3 - k, 0)[HALO:]
        return pre

    def prepare(ref, taps, act, act_t, slo):
        pre = conv(ref, pl.ds(0, ST), taps[...])
        sig = sigmoid(pre)
        slo[...] = sig * (1.0 + pre * (1.0 - sig))
        value = (pre * sig).astype(BF)
        act[...] = value
        for b in range(NB):
            act_t[b] = jnp.transpose(value[b * BLOCK : (b + 1) * BLOCK].astype(F32)).astype(BF)

    prepare(bp, kb, act_b, bt, slope_b)

    def row_peer(r):
        return y * 4 + (x + r) % 4

    def f1(r, k):
        return remote(
            sf.at[((x + r) % 4) * 2 + k], rf.at[x * 2 + k], f1s.at[r, k], f1r.at[r, k], row_peer(r)
        )

    def b1(r, k):
        return remote(
            sb.at[((x + r) % 4) * 2 + k], rb.at[x * 2 + k], b1s.at[r, k], b1r.at[r, k], row_peer(r)
        )

    def f2(r, k):
        return remote(
            of.at[((x + r) % 4) * 2 + k], inf.at[x * 2 + k], f2s.at[r, k], f2r.at[r, k], row_peer(r)
        )

    def b2(r, k):
        return remote(
            ob.at[((x + r) % 4) * 2 + k], inb.at[x * 2 + k], b2s.at[r, k], b2r.at[r, k], row_peer(r)
        )

    def yf_cp(r, k):
        return remote(
            tf.at[k], yf.at[y * 2 + k], yfs.at[r, k], yfr.at[y, k], ((y + r) % 4) * 4 + x
        )

    def yb_cp(r, k):
        return remote(
            tb.at[k], yb.at[y * 2 + k], ybs.at[r, k], ybr.at[y, k], ((y + r) % 4) * 4 + x
        )

    def forward_local(p, carry):
        r, k, q = order(p)
        lanes = lanes_of(q)
        pre = conv(xp, lanes, kx[:, lanes])
        slope[q] = pre
        act = (pre * sigmoid(pre)).astype(BF).astype(F32)
        scaled = (act * acc_g[q]).astype(BF)
        sx[q] = scaled
        weighted = (scaled.astype(F32) * acc_o[q]).astype(BF)
        wx[q] = weighted
        state = None
        total = None
        for b in range(NB):
            tot_b = tot[q, pl.ds(b, 1), :]
            grown = dot(bt[b], weighted[b * BLOCK : (b + 1) * BLOCK])
            if b == 0:
                state, total = grown, tot_b
            else:
                ls[q, b - 1] = state
                state = jnp.exp(tot_b) * state + grown
                total = total + tot_b
        state = state.astype(BF)
        tail = tail_rows(total)

        @pl.when(r == 0)
        def _():
            rf[q, 0:ST, :] = state
            rf[q, ST:LROWS, :] = tail

        @pl.when(r > 0)
        def _():
            sf[q, 0:ST, :] = state
            sf[q, ST:LROWS, :] = tail
            f1(r, k).start()

        return carry

    lax.fori_loop(0, 3, forward_local, 0)
    lax.fori_loop(3, NQ, spread, 0)
    lax.fori_loop(3, NQ, forward_local, 0)

    prepare(cp, kc, act_c, ct, slope_c)

    def backward_local(p, carry):
        r, k, q = order(p)
        lanes = lanes_of(q)
        state = None
        for b in reversed(range(NB)):
            grads = (gs[blk(b), lanes].astype(F32) * growth[q, blk(b), :]).astype(BF)
            gw[q, blk(b), :] = grads
            grown = dot(ct[b], grads)
            if b == NB - 1:
                state = grown
            else:
                la[q, b] = state
                state = jnp.exp(tot[q, pl.ds(b, 1), :]) * state + grown
        state = state.astype(BF)

        @pl.when(r == 0)
        def _():
            rb[q] = state

        @pl.when(r > 0)
        def _():
            sb[q] = state
            b1(r, k).start()

        return carry

    lax.fori_loop(0, NQ, backward_local, 0)

    for b in range(NB):
        scores = dot_nt(act_c[blk(b), :], act_b[blk(b), :])
        sl[b] = scores * lower_f
        su[b] = jnp.transpose(scores) * upper_f

    left = lax.broadcasted_iota(jnp.int32, (BLOCK, BLOCK), 1) < 64

    def halves(value):
        zero = jnp.zeros_like(value)
        return jnp.concatenate([jnp.where(left, value, zero), jnp.where(left, zero, value)], axis=0)

    def intra(q, carry):
        depth = lax.broadcasted_iota(jnp.int32, (6 * H, 2 * W), 0)
        col = lax.broadcasted_iota(jnp.int32, (6 * H, 2 * W), 1)
        hit = (depth % H == 4 * q + col // BLOCK) & (depth < 3 * H)
        hit = hit.astype(F32).astype(BF)
        for b in range(NB):
            down = dot(lh[blk(b), :], hit)
            for pair in range(2):
                part = pl.ds(pair * BLOCK, BLOCK)
                across = jnp.concatenate(
                    [cumt[q, pl.ds(2 * pair + i, 1), blk(b)] for i in range(2)], axis=1
                )
                differ = down[:, pair * W : (pair + 1) * W] - across
                table = jnp.exp(-jnp.abs(differ))
                scores = jnp.concatenate([sl[b], sl[b]], axis=1)
                scores_t = jnp.concatenate([su[b], su[b]], axis=1)
                mixing = (table * scores).astype(BF)
                mixing_t = (table * scores_t).astype(BF)
                scaled = sx[q, blk(b), part]
                grads = gs[blk(b), pl.ds(pl.multiple_of(q * W + pair * BLOCK, BLOCK), BLOCK)]
                wide_x = halves(scaled)
                pre = slope[q, blk(b), part]
                sig = sigmoid(pre)
                slope[q, blk(b), part] = sig * (1.0 + pre * (1.0 - sig))
                direct = ske[q, 0:1, part] * (pre * sig).astype(BF).astype(F32)
                acc_o[q, blk(b), part] = direct + dot(mixing, wide_x)
                inner = dot(mixing_t, halves(grads))
                acc_g[q, blk(b), part] = (
                    acc_g[q, blk(b), part] * inner + ske[q, 0:1, part] * grads.astype(F32)
                )
                both = table * dot_nt(grads, wide_x)
                ps[b] += both[:, :BLOCK] + both[:, BLOCK:]
        return carry

    def row_forward(k):
        state, total = None, None
        for i in range(4):
            local = rf[i * 2 + k, 0:ST, :].astype(F32)
            own = tail_sum(rf[i * 2 + k, ST:LROWS, :])
            if i == 0:
                state, total = local, own
            else:
                state = jnp.exp(own) * state + local
                total = total + own
        tf[k, 0:ST, :] = state.astype(BF)
        tf[k, ST:LROWS, :] = tail_rows(total)
        rs_f[k] = jnp.zeros((ST, W), F32)
        for r in range(1, 4):
            @pl.when(y + r <= 3)
            def _():
                yf_cp(r, k).start()

    def row_backward(k):
        state = None
        for i in reversed(range(4)):
            local = rb[i * 2 + k].astype(F32)
            own = tail_sum(rf[i * 2 + k, ST:LROWS, :])
            state = local if i == 3 else jnp.exp(own) * state + local
        tb[k, 0:ST, :] = state.astype(BF)
        tb[k, ST:LROWS, :] = tf[k, ST:LROWS, :]
        rs_b[k] = jnp.zeros((ST, W), F32)
        for r in range(1, 4):
            @pl.when(y - (4 - r) >= 0)
            def _():
                yb_cp(r, k).start()

    def finish_forward(k):
        for i in range(3):
            @pl.when(i < y)
            def _():
                remote(
                    tf.at[k], yf.at[i * 2 + k], yfs.at[1, k], yfr.at[i, k], nxt
                ).wait_recv()
                own = tail_sum(yf[i * 2 + k, ST:LROWS, :])
                rs_f[k] = jnp.exp(own) * rs_f[k] + yf[i * 2 + k, 0:ST, :].astype(F32)
        state = rs_f[k]
        for i in range(4):
            out = state.astype(BF)
            of[i * 2 + k] = out

            @pl.when(x == i)
            def _():
                inf[i * 2 + k] = out

            if i < 3:
                own = tail_sum(rf[i * 2 + k, ST:LROWS, :])
                state = jnp.exp(own) * state + rf[i * 2 + k, 0:ST, :].astype(F32)
        for r in range(1, 4):
            f2(r, k).start()

    def finish_backward(k):
        for i in reversed(range(1, 4)):
            @pl.when(i > y)
            def _():
                remote(
                    tb.at[k], yb.at[i * 2 + k], ybs.at[1, k], ybr.at[i, k], nxt
                ).wait_recv()
                own = tail_sum(yb[i * 2 + k, ST:LROWS, :])
                rs_b[k] = jnp.exp(own) * rs_b[k] + yb[i * 2 + k, 0:ST, :].astype(F32)
        state = rs_b[k]
        for i in reversed(range(4)):
            out = state.astype(BF)
            ob[i * 2 + k] = out

            @pl.when(x == i)
            def _():
                inb[i * 2 + k] = out

            if i > 0:
                own = tail_sum(rf[i * 2 + k, ST:LROWS, :])
                state = jnp.exp(own) * state + rb[i * 2 + k].astype(F32)
        for r in range(1, 4):
            b2(r, k).start()

    def take_forward(k):
        for r in range(1, 4):
            f1(r, k).wait_recv()
        row_forward(k)

    def take_backward(k):
        for r in range(1, 4):
            b1(r, k).wait_recv()
        row_backward(k)

    def order_in(p):
        r = p % 4
        k = p // 4
        return r, k, ((x + 4 - r) % 4) * 2 + k

    def out_copy(q):
        return pltpu.make_async_copy(sx.at[q], out_hbm.at[:, lanes_of(q)], out_sem.at[0, q])

    def gp_copy(q):
        lanes = lanes_of(q)
        return pltpu.make_async_copy(gs.at[:, lanes], gp_hbm.at[:, lanes], out_sem.at[1, q])

    def enter_forward(p, carry):
        r, k, q = order_in(p)

        @pl.when(r > 0)
        def _():
            f2(r, k).wait_recv()

        start = inf[q]
        base = start.astype(F32)
        total = None
        for b in range(NB):
            if b > 0:
                tot_b = tot[q, pl.ds(b - 1, 1), :]
                total = tot_b if b == 1 else total + tot_b
                start = (ls[q, b - 1] + jnp.exp(total) * base).astype(BF)
            carried = growth[q, blk(b), :] * dot(act_c[blk(b), :], start)
            sx[q, blk(b), :] = (acc_o[q, blk(b), :] + carried).astype(BF)
            grad_c[blk(b), :] += dot_nt(gw[q, blk(b), :], start)
        out_copy(q).start()
        return carry

    take_forward(0)
    lax.fori_loop(0, 3, intra, 0)
    take_forward(1)
    lax.fori_loop(3, 6, intra, 0)
    finish_forward(0)
    take_backward(0)
    lax.fori_loop(6, 7, intra, 0)
    finish_forward(1)
    take_backward(1)
    lax.fori_loop(7, NQ, intra, 0)
    finish_backward(0)
    lax.fori_loop(0, 4, enter_forward, 0)
    finish_backward(1)
    lax.fori_loop(4, NQ, enter_forward, 0)

    tail = pl.ds(T, HALO)

    def ghalo(src, dst, slot):
        return remote(src, dst, ghalo_s.at[slot], ghalo_r.at[slot], prv)

    def ghalo_x(q):
        return ghalo(gs.at[head, lanes_of(q)], gh.at[q], q)

    def ghalo_b():
        return ghalo(gpb.at[head], gpb.at[tail], NQ)

    def ghalo_c():
        return ghalo(gpc.at[head], gpc.at[tail], NQ + 1)

    def send_halo(copy):
        @pl.when(me > 0)
        def _():
            copy.start()

    def take_halo(copy, dst):
        @pl.when(me < 15)
        def _():
            copy.wait_recv()

        @pl.when(me == 15)
        def _():
            dst[...] = jnp.zeros((HALO, W), BF)

    def enter_backward(p, carry):
        r, k, q = order_in(p)

        @pl.when(r > 0)
        def _():
            b2(r, k).wait_recv()

        after = inb[q]
        base = after.astype(F32)
        total = None
        for b in reversed(range(NB)):
            if b < NB - 1:
                tot_b = tot[q, pl.ds(b + 1, 1), :]
                total = tot_b if b == NB - 2 else total + tot_b
                after = (la[q, b] + jnp.exp(total) * base).astype(BF)
            outer = stte[q, blk(b), :] * dot(act_b[blk(b), :], after)
            grads = (acc_g[q, blk(b), :] + outer) * slope[q, blk(b), :]
            gs[blk(b), lanes_of(q)] = grads.astype(BF)
            grad_b[blk(b), :] += dot_nt(wx[q, blk(b), :], after)
        send_halo(ghalo_x(q))
        gp_copy(q).start()
        return carry

    for b in range(NB):
        pair_sum = ps[b] * lower_f
        pair_t = jnp.transpose(pair_sum).astype(BF)
        grad_b[blk(b), :] = dot(pair_t, act_c[blk(b), :])
        into_c = grad_c[blk(b), :] + dot(pair_sum.astype(BF), act_b[blk(b), :])
        gpc[blk(b), :] = (into_c * slope_c[blk(b), :]).astype(BF)
    send_halo(ghalo_c())
    gpc_out[pl.ds(0, T), :] = gpc[pl.ds(0, T), :]

    lax.fori_loop(0, NQ, enter_backward, 0)

    for b in range(NB):
        gpb[blk(b), :] = (grad_b[blk(b), :] * slope_b[blk(b), :]).astype(BF)
    send_halo(ghalo_b())
    gpb_out[pl.ds(0, T), :] = gpb[pl.ds(0, T), :]
    for q in range(NQ):
        take_halo(ghalo_x(q), gh.at[q])
        gh_out[:, q * W : (q + 1) * W] = gh[q]
    for ref, out, copy in ((gpb, gpb_out, ghalo_b()), (gpc, gpc_out, ghalo_c())):
        take_halo(copy, ref.at[tail])
        out[tail, :] = ref[tail, :]

    for q in range(NQ):
        out_copy(q).wait()
        gp_copy(q).wait()

    @pl.when(me < 15)
    def _():
        for h in halos:
            h.wait_send()

    @pl.when(me > 0)
    def _():
        for q in range(NQ):
            ghalo_x(q).wait_send()
        ghalo_b().wait_send()
        ghalo_c().wait_send()

    for k in range(2):
        for r in range(1, 4):
            f1(r, k).wait_send()
            b1(r, k).wait_send()
            f2(r, k).wait_send()
            b2(r, k).wait_send()

            @pl.when(y + r <= 3)
            def _():
                yf_cp(r, k).wait_send()

            @pl.when(y - (4 - r) >= 0)
            def _():
                yb_cp(r, k).wait_send()


def back_kernel(
    out_hbm, gp_hbm, gh_hbm, gpb_hbm, gpc_hbm, kx, kb, kc, out_ref, gx_ref, gb_ref, gc_ref,
    out_v, gp_v, gx_v, gpb, gpc, gb_v, gc_v, in_sem, out_sem,
):
    def rows(i):
        return pl.ds(i * BLOCK, BLOCK)

    loads = [pltpu.make_async_copy(gh_hbm, gp_v.at[pl.ds(T, HALO)], in_sem.at[2 * NB])]
    for i in reversed(range(NB)):
        loads.append(pltpu.make_async_copy(gp_hbm.at[rows(i)], gp_v.at[rows(i)], in_sem.at[i]))
    loads.append(pltpu.make_async_copy(gpb_hbm, gpb, in_sem.at[2 * NB + 1]))
    loads.append(pltpu.make_async_copy(gpc_hbm, gpc, in_sem.at[2 * NB + 2]))
    passed = [
        pltpu.make_async_copy(out_hbm.at[rows(i)], out_v.at[rows(i)], in_sem.at[NB + i])
        for i in range(NB)
    ]
    for copy in loads + passed:
        copy.start()

    def back(value, taps, count):
        value = value.astype(F32)
        size = value.shape[0]
        grad = taps[3:4] * value[:count]
        for k in range(3):
            grad = grad + taps[k : k + 1] * pltpu.roll(value, size - (3 - k), 0)[:count]
        return grad.astype(BF)

    stores = []

    def store(src, dst, slot):
        stores.append(pltpu.make_async_copy(src, dst, out_sem.at[slot]))
        stores[-1].start()

    loads[0].wait()
    for i in reversed(range(NB)):
        loads[NB - i].wait()

        def slab(q, carry):
            lanes = pl.ds(pl.multiple_of(q * W, W), W)
            value = gp_v[pl.ds(i * BLOCK, BLOCK + HALO), lanes]
            gx_v[rows(i), lanes] = back(value, kx[:, lanes], BLOCK)
            return carry

        lax.fori_loop(0, NQ, slab, 0)
        store(gx_v.at[rows(i)], gx_ref.at[rows(i)], i)
        if i % 2 == 1:
            for j in (i - 1, i):
                passed[j].wait()
                store(out_v.at[rows(j)], out_ref.at[rows(j)], NB + j)
    loads[NB + 1].wait()
    gb_v[...] = back(gpb[...], kb[...], T)
    store(gb_v, gb_ref, 2 * NB)
    loads[NB + 2].wait()
    gc_v[...] = back(gpc[...], kc[...], T)
    store(gc_v, gc_ref, 2 * NB + 1)
    for copy in stores:
        copy.wait()


def on_device(x, b, c, kx, kb, kc, step, dlog, skip, g):
    hbm = pl.BlockSpec(memory_space=pl.ANY)
    vmem = pl.BlockSpec(memory_space=pltpu.VMEM)
    dma = pltpu.SemaphoreType.DMA
    full = (NQ, T, W)
    scratch = [
        pltpu.VMEM((T + HALO, NQ * W), BF),
        pltpu.VMEM((T + HALO, ST), BF),
        pltpu.VMEM((T + HALO, ST), BF),
        pltpu.VMEM((T, NQ * W), BF),
        pltpu.VMEM((T + 16, 6 * H), BF),
        pltpu.VMEM((NQ, 8, T), F32),
        pltpu.VMEM((T + 16, 2 * W), F32),
        pltpu.VMEM((NQ, 8, W), F32),
        pltpu.VMEM((NQ, 8, W), F32),
        pltpu.VMEM(full, F32),
        pltpu.VMEM(full, F32),
        pltpu.VMEM(full, F32),
        pltpu.VMEM(full, F32),
        pltpu.VMEM(full, F32),
        pltpu.VMEM(full, BF),
        pltpu.VMEM(full, BF),
        pltpu.VMEM(full, BF),
        pltpu.VMEM((NQ, 3, ST, W), F32),
        pltpu.VMEM((NQ, 3, ST, W), F32),
        pltpu.VMEM((NQ, HALO, W), BF),
        pltpu.VMEM((T + HALO, ST), BF),
        pltpu.VMEM((T + HALO, ST), BF),
        pltpu.VMEM((T, ST), BF),
        pltpu.VMEM((T, ST), BF),
        pltpu.VMEM((NB, ST, BLOCK), BF),
        pltpu.VMEM((NB, ST, BLOCK), BF),
        pltpu.VMEM((T, ST), F32),
        pltpu.VMEM((T, ST), F32),
        pltpu.VMEM((NB, BLOCK, BLOCK), F32),
        pltpu.VMEM((NB, BLOCK, BLOCK), F32),
        pltpu.VMEM((NB, BLOCK, BLOCK), F32),
        pltpu.VMEM((T, ST), F32),
        pltpu.VMEM((T, ST), F32),
        pltpu.VMEM((NQ, LROWS, W), BF),
        pltpu.VMEM((NQ, ST, W), BF),
        pltpu.VMEM((NQ, LROWS, W), BF),
        pltpu.VMEM((NQ, ST, W), BF),
        pltpu.VMEM((2, LROWS, W), BF),
        pltpu.VMEM((2, LROWS, W), BF),
        pltpu.VMEM((NQ, LROWS, W), BF),
        pltpu.VMEM((NQ, LROWS, W), BF),
        pltpu.VMEM((NQ, ST, W), BF),
        pltpu.VMEM((NQ, ST, W), BF),
        pltpu.VMEM((NQ, ST, W), BF),
        pltpu.VMEM((NQ, ST, W), BF),
        pltpu.VMEM((2, ST, W), F32),
        pltpu.VMEM((2, ST, W), F32),
        dma((4,)), dma((2, NQ)), dma((3,)), dma((3,)), dma((10,)), dma((10,)),
    ] + [dma((4, 2))] * 12
    out, gp, gh, gpb, gpc = pl.pallas_call(
        kernel,
        out_shape=(
            jax.ShapeDtypeStruct(x.shape, BF),
            jax.ShapeDtypeStruct(x.shape, BF),
            jax.ShapeDtypeStruct((HALO, NQ * W), BF),
            jax.ShapeDtypeStruct((T + HALO, ST), BF),
            jax.ShapeDtypeStruct((T + HALO, ST), BF),
        ),
        in_specs=[hbm] * 3 + [vmem] * 6 + [hbm],
        out_specs=(hbm, hbm, vmem, vmem, vmem),
        scratch_shapes=scratch,
        compiler_params=pltpu.CompilerParams(
            collective_id=0, has_side_effects=True, vmem_limit_bytes=67043328
        ),
    )(x, b, c, kx, kb, kc, step.T, dlog.reshape(1, H), skip.reshape(1, H), g)
    return pl.pallas_call(
        back_kernel,
        out_shape=(
            jax.ShapeDtypeStruct(x.shape, BF),
            jax.ShapeDtypeStruct(x.shape, BF),
            jax.ShapeDtypeStruct(b.shape, BF),
            jax.ShapeDtypeStruct(c.shape, BF),
        ),
        in_specs=[hbm] * 5 + [vmem] * 3,
        out_specs=(hbm,) * 4,
        scratch_shapes=[
            pltpu.VMEM((T, NQ * W), BF),
            pltpu.VMEM((T + HALO, NQ * W), BF),
            pltpu.VMEM((T, NQ * W), BF),
            pltpu.VMEM((T + HALO, ST), BF),
            pltpu.VMEM((T + HALO, ST), BF),
            pltpu.VMEM((T, ST), BF),
            pltpu.VMEM((T, ST), BF),
            dma((2 * NB + 3,)),
            dma((2 * NB + 2,)),
        ],
    )(out, gp, gh, gpb, gpc, kx, kb, kc)


def solution(mesh):
    rows = P(("doc", "context"), "head")
    taps = P(None, "head")
    return jax.shard_map(
        on_device,
        mesh=mesh,
        in_specs=(rows, rows, rows, taps, taps, taps, rows, P("head"), P("head"), rows),
        out_specs=(rows, rows, rows, rows),
        check_vma=False,
    )
```

```python
import jax
import jax.numpy as jnp
from jax import lax
from jax.experimental import pallas as pl
from jax.experimental.pallas import tpu as pltpu
from jax.sharding import PartitionSpec as P

BLOCK = 128
NB = 4
T = 512
H = 32
W = 256
NQ = 8
ST = 256
HALO = 16
LROWS = ST + HALO
MESH = pl.DeviceIdType.MESH
F32 = jnp.float32
BF = jnp.bfloat16


def dot(a, b):
    return jnp.dot(a, b, preferred_element_type=F32)


def dot_nt(a, b):
    return lax.dot_general(a, b, (((1,), (1,)), ((), ())), preferred_element_type=F32)


def split3(v):
    hi = v.astype(BF)
    rest = v - hi.astype(F32)
    mid = rest.astype(BF)
    low = (rest - mid.astype(F32)).astype(BF)
    return hi, mid, low


def sigmoid(v):
    return 1.0 / (1.0 + jnp.exp(-v))


def tail_rows(row):
    hi, mid, low = split3(row)
    index = lax.broadcasted_iota(jnp.int32, (HALO, row.shape[1]), 0)
    zero = jnp.zeros((HALO, row.shape[1]), F32)
    full = jnp.where(
        index == 0,
        hi.astype(F32),
        jnp.where(index == 1, mid.astype(F32), jnp.where(index == 2, low.astype(F32), zero)),
    )
    return full.astype(BF)


def tail_sum(rows):
    return jnp.sum(rows.astype(F32), axis=0, keepdims=True)


def kernel(
    x_hbm, b_hbm, c_hbm, kx, kb, kc, step, dlog, skip, g_hbm,
    out_hbm, gp_hbm, gh_out, gpb_out, gpc_out,
    xp, bp, cp, gs, lh, cumt, ex, tot, ske,
    slope, growth, stte, acc_o, acc_g, sx, wx, gw, ls, la,
    gh, gpb, gpc, act_b, act_c, bt, ct, slope_b, slope_c,
    ps, sl, su, grad_b, grad_c,
    sf, sb, rf, rb, tf, tb, yf, yb, of, ob, inf, inb, rs_f, rs_b,
    in_sem, out_sem, halo_s, halo_r, ghalo_s, ghalo_r,
    f1s, f1r, b1s, b1r, yfs, yfr, ybs, ybr, f2s, f2r, b2s, b2r,
):
    me = lax.axis_index("context")
    y = me // 4
    x = me % 4
    nxt = (me + 1) % 16
    prv = (me + 15) % 16

    def remote(src, dst, s, r, peer):
        return pltpu.make_async_remote_copy(
            src_ref=src, dst_ref=dst, send_sem=s, recv_sem=r,
            device_id={"context": peer}, device_id_type=MESH,
        )

    barrier = pltpu.get_barrier_semaphore()
    peers = [nxt, prv]
    peers += [y * 4 + (x + r) % 4 for r in range(1, 4)]
    peers += [((y + r) % 4) * 4 + x for r in range(1, 4)]
    for peer in peers:
        pl.semaphore_signal(barrier, inc=1, device_id={"context": peer}, device_id_type=MESH)

    body = pl.ds(HALO, T)
    loads = [
        pltpu.make_async_copy(b_hbm, bp.at[body], in_sem.at[0]),
        pltpu.make_async_copy(c_hbm, cp.at[body], in_sem.at[1]),
        pltpu.make_async_copy(x_hbm, xp.at[body], in_sem.at[2]),
        pltpu.make_async_copy(g_hbm, gs, in_sem.at[3]),
    ]
    for load in loads:
        load.start()

    rate = -jnp.exp(jnp.transpose(jnp.broadcast_to(dlog[...], (8, H)))[:, 0:1])
    lower = (
        lax.broadcasted_iota(jnp.int32, (BLOCK, BLOCK), 0)
        >= lax.broadcasted_iota(jnp.int32, (BLOCK, BLOCK), 1)
    )
    lower_f = lower.astype(F32)
    upper_f = (
        lax.broadcasted_iota(jnp.int32, (BLOCK, BLOCK), 0)
        <= lax.broadcasted_iota(jnp.int32, (BLOCK, BLOCK), 1)
    ).astype(F32)
    upper_b = upper_f.astype(BF)
    for b in range(NB):
        rows = pl.ds(b * BLOCK, BLOCK)
        step_b = step[:, rows]
        logs = split3(step_b * rate)
        flipped = dot(logs[0], upper_b) + dot(logs[1], upper_b) + dot(logs[2], upper_b)
        for q in range(NQ):
            cumt[q, 0:4, rows] = flipped[4 * q : 4 * q + 4]
        pieces = split3(jnp.transpose(flipped)) + split3(jnp.transpose(step_b))
        lh[rows, :] = jnp.concatenate([p.astype(F32) for p in pieces], axis=1).astype(BF)
    skips = split3(jnp.broadcast_to(skip[...], (16, H)))
    zero_s = jnp.zeros((16, 3 * H), F32)
    lh[pl.ds(T, 16), :] = jnp.concatenate(
        [p.astype(F32) for p in skips] + [zero_s], axis=1
    ).astype(BF)
    ps[...] = jnp.zeros_like(ps)
    grad_c[...] = jnp.zeros_like(grad_c)

    pl.semaphore_wait(barrier, 8)

    head = pl.ds(0, HALO)
    last = pl.ds(T - HALO, HALO)
    halos = [
        remote(b_hbm.at[last], bp.at[head], halo_s.at[0], halo_r.at[0], nxt),
        remote(c_hbm.at[last], cp.at[head], halo_s.at[1], halo_r.at[1], nxt),
        remote(x_hbm.at[last], xp.at[head], halo_s.at[2], halo_r.at[2], nxt),
    ]

    @pl.when(me < 15)
    def _():
        for h in halos:
            h.start()

    @pl.when(me == 0)
    def _():
        for ref in (bp, cp, xp):
            ref[head, :] = jnp.zeros((HALO, ref.shape[1]), BF)

    def blk(b):
        return pl.ds(b * BLOCK, BLOCK)

    def lanes_of(q):
        return pl.ds(pl.multiple_of(q * W, W), W)

    def order(p):
        far = p < 6
        r = jnp.where(far, jnp.where(p % 3 == 0, 2, jnp.where(p % 3 == 1, 1, 3)), 0)
        k = jnp.where(far, p // 3, p - 6)
        return r, k, ((x + r) % 4) * 2 + k

    def spread(p, carry):
        q = order(p)[2]
        depth = lax.broadcasted_iota(jnp.int32, (6 * H, 2 * W), 0)
        col = lax.broadcasted_iota(jnp.int32, (6 * H, 2 * W), 1)
        hit = (depth % H == 4 * q + (col % W) // 64) & ((depth // (3 * H)) == (col // W))
        ex[...] = dot(lh[...], hit.astype(F32).astype(BF))
        ske[q] = ex[pl.ds(T, 8), 0:W]
        for b in range(NB):
            cum = ex[blk(b), 0:W]
            steps = ex[blk(b), W : 2 * W]
            tot_b = ex[pl.ds(b * BLOCK + BLOCK - 1, 1), 0:W]
            tot[q, pl.ds(b, 1), :] = tot_b
            to_end = jnp.exp(tot_b - cum)
            growth[q, blk(b), :] = jnp.exp(cum)
            acc_o[q, blk(b), :] = to_end
            acc_g[q, blk(b), :] = steps
            stte[q, blk(b), :] = steps * to_end
        return carry

    lax.fori_loop(0, 3, spread, 0)

    for load in loads:
        load.wait()

    @pl.when(me > 0)
    def _():
        for h in halos:
            h.wait_recv()

    def conv(ref, lanes, taps):
        padded = ref[:, lanes].astype(F32)
        pre = taps[3:4] * padded[HALO:]
        for k in range(3):
            pre = pre + taps[k : k + 1] * pltpu.roll(padded, 3 - k, 0)[HALO:]
        return pre

    def prepare(ref, taps, act, act_t, slo):
        pre = conv(ref, pl.ds(0, ST), taps[...])
        sig = sigmoid(pre)
        slo[...] = sig * (1.0 + pre * (1.0 - sig))
        value = (pre * sig).astype(BF)
        act[...] = value
        for b in range(NB):
            act_t[b] = jnp.transpose(value[b * BLOCK : (b + 1) * BLOCK].astype(F32)).astype(BF)

    prepare(bp, kb, act_b, bt, slope_b)

    def row_peer(r):
        return y * 4 + (x + r) % 4

    def f1(r, k):
        return remote(
            sf.at[((x + r) % 4) * 2 + k], rf.at[x * 2 + k], f1s.at[r, k], f1r.at[r, k], row_peer(r)
        )

    def b1(r, k):
        return remote(
            sb.at[((x + r) % 4) * 2 + k], rb.at[x * 2 + k], b1s.at[r, k], b1r.at[r, k], row_peer(r)
        )

    def f2(r, k):
        return remote(
            of.at[((x + r) % 4) * 2 + k], inf.at[x * 2 + k], f2s.at[r, k], f2r.at[r, k], row_peer(r)
        )

    def b2(r, k):
        return remote(
            ob.at[((x + r) % 4) * 2 + k], inb.at[x * 2 + k], b2s.at[r, k], b2r.at[r, k], row_peer(r)
        )

    def yf_cp(r, k):
        return remote(
            tf.at[k], yf.at[y * 2 + k], yfs.at[r, k], yfr.at[y, k], ((y + r) % 4) * 4 + x
        )

    def yb_cp(r, k):
        return remote(
            tb.at[k], yb.at[y * 2 + k], ybs.at[r, k], ybr.at[y, k], ((y + r) % 4) * 4 + x
        )

    def forward_local(p, carry):
        r, k, q = order(p)
        lanes = lanes_of(q)
        pre = conv(xp, lanes, kx[:, lanes])
        slope[q] = pre
        act = (pre * sigmoid(pre)).astype(BF).astype(F32)
        scaled = (act * acc_g[q]).astype(BF)
        sx[q] = scaled
        weighted = (scaled.astype(F32) * acc_o[q]).astype(BF)
        wx[q] = weighted
        state = None
        total = None
        for b in range(NB):
            tot_b = tot[q, pl.ds(b, 1), :]
            grown = dot(bt[b], weighted[b * BLOCK : (b + 1) * BLOCK])
            if b == 0:
                state, total = grown, tot_b
            else:
                ls[q, b - 1] = state
                state = jnp.exp(tot_b) * state + grown
                total = total + tot_b
        state = state.astype(BF)
        tail = tail_rows(total)

        @pl.when(r == 0)
        def _():
            rf[q, 0:ST, :] = state
            rf[q, ST:LROWS, :] = tail

        @pl.when(r > 0)
        def _():
            sf[q, 0:ST, :] = state
            sf[q, ST:LROWS, :] = tail
            f1(r, k).start()

        return carry

    lax.fori_loop(0, 3, forward_local, 0)
    lax.fori_loop(3, NQ, spread, 0)
    lax.fori_loop(3, NQ, forward_local, 0)

    prepare(cp, kc, act_c, ct, slope_c)

    def backward_local(p, carry):
        r, k, q = order(p)
        lanes = lanes_of(q)
        state = None
        for b in reversed(range(NB)):
            grads = (gs[blk(b), lanes].astype(F32) * growth[q, blk(b), :]).astype(BF)
            gw[q, blk(b), :] = grads
            grown = dot(ct[b], grads)
            if b == NB - 1:
                state = grown
            else:
                la[q, b] = state
                state = jnp.exp(tot[q, pl.ds(b, 1), :]) * state + grown
        state = state.astype(BF)

        @pl.when(r == 0)
        def _():
            rb[q] = state

        @pl.when(r > 0)
        def _():
            sb[q] = state
            b1(r, k).start()

        return carry

    lax.fori_loop(0, NQ, backward_local, 0)

    for b in range(NB):
        scores = dot_nt(act_c[blk(b), :], act_b[blk(b), :])
        sl[b] = scores * lower_f
        su[b] = jnp.transpose(scores) * upper_f

    left = lax.broadcasted_iota(jnp.int32, (BLOCK, BLOCK), 1) < 64

    def halves(value):
        zero = jnp.zeros_like(value)
        return jnp.concatenate([jnp.where(left, value, zero), jnp.where(left, zero, value)], axis=0)

    def intra(q, carry):
        depth = lax.broadcasted_iota(jnp.int32, (6 * H, 2 * W), 0)
        col = lax.broadcasted_iota(jnp.int32, (6 * H, 2 * W), 1)
        hit = (depth % H == 4 * q + col // BLOCK) & (depth < 3 * H)
        hit = hit.astype(F32).astype(BF)
        for b in range(NB):
            down = dot(lh[blk(b), :], hit)
            for pair in range(2):
                part = pl.ds(pair * BLOCK, BLOCK)
                across = jnp.concatenate(
                    [cumt[q, pl.ds(2 * pair + i, 1), blk(b)] for i in range(2)], axis=1
                )
                differ = down[:, pair * W : (pair + 1) * W] - across
                table = jnp.exp(-jnp.abs(differ))
                scores = jnp.concatenate([sl[b], sl[b]], axis=1)
                scores_t = jnp.concatenate([su[b], su[b]], axis=1)
                mixing = (table * scores).astype(BF)
                mixing_t = (table * scores_t).astype(BF)
                scaled = sx[q, blk(b), part]
                grads = gs[blk(b), pl.ds(pl.multiple_of(q * W + pair * BLOCK, BLOCK), BLOCK)]
                wide_x = halves(scaled)
                pre = slope[q, blk(b), part]
                sig = sigmoid(pre)
                slope[q, blk(b), part] = sig * (1.0 + pre * (1.0 - sig))
                direct = ske[q, 0:1, part] * (pre * sig).astype(BF).astype(F32)
                acc_o[q, blk(b), part] = direct + dot(mixing, wide_x)
                inner = dot(mixing_t, halves(grads))
                acc_g[q, blk(b), part] = (
                    acc_g[q, blk(b), part] * inner + ske[q, 0:1, part] * grads.astype(F32)
                )
                both = table * dot_nt(grads, wide_x)
                ps[b] += both[:, :BLOCK] + both[:, BLOCK:]
        return carry

    def row_forward(k):
        state, total = None, None
        for i in range(4):
            local = rf[i * 2 + k, 0:ST, :].astype(F32)
            own = tail_sum(rf[i * 2 + k, ST:LROWS, :])
            if i == 0:
                state, total = local, own
            else:
                state = jnp.exp(own) * state + local
                total = total + own
        tf[k, 0:ST, :] = state.astype(BF)
        tf[k, ST:LROWS, :] = tail_rows(total)
        rs_f[k] = jnp.zeros((ST, W), F32)
        for r in range(1, 4):
            @pl.when(y + r <= 3)
            def _():
                yf_cp(r, k).start()

    def row_backward(k):
        state = None
        for i in reversed(range(4)):
            local = rb[i * 2 + k].astype(F32)
            own = tail_sum(rf[i * 2 + k, ST:LROWS, :])
            state = local if i == 3 else jnp.exp(own) * state + local
        tb[k, 0:ST, :] = state.astype(BF)
        tb[k, ST:LROWS, :] = tf[k, ST:LROWS, :]
        rs_b[k] = jnp.zeros((ST, W), F32)
        for r in range(1, 4):
            @pl.when(y - (4 - r) >= 0)
            def _():
                yb_cp(r, k).start()

    def finish_forward(k):
        for i in range(3):
            @pl.when(i < y)
            def _():
                remote(
                    tf.at[k], yf.at[i * 2 + k], yfs.at[1, k], yfr.at[i, k], nxt
                ).wait_recv()
                own = tail_sum(yf[i * 2 + k, ST:LROWS, :])
                rs_f[k] = jnp.exp(own) * rs_f[k] + yf[i * 2 + k, 0:ST, :].astype(F32)
        state = rs_f[k]
        for i in range(4):
            out = state.astype(BF)
            of[i * 2 + k] = out

            @pl.when(x == i)
            def _():
                inf[i * 2 + k] = out

            if i < 3:
                own = tail_sum(rf[i * 2 + k, ST:LROWS, :])
                state = jnp.exp(own) * state + rf[i * 2 + k, 0:ST, :].astype(F32)
        for r in range(1, 4):
            f2(r, k).start()

    def finish_backward(k):
        for i in reversed(range(1, 4)):
            @pl.when(i > y)
            def _():
                remote(
                    tb.at[k], yb.at[i * 2 + k], ybs.at[1, k], ybr.at[i, k], nxt
                ).wait_recv()
                own = tail_sum(yb[i * 2 + k, ST:LROWS, :])
                rs_b[k] = jnp.exp(own) * rs_b[k] + yb[i * 2 + k, 0:ST, :].astype(F32)
        state = rs_b[k]
        for i in reversed(range(4)):
            out = state.astype(BF)
            ob[i * 2 + k] = out

            @pl.when(x == i)
            def _():
                inb[i * 2 + k] = out

            if i > 0:
                own = tail_sum(rf[i * 2 + k, ST:LROWS, :])
                state = jnp.exp(own) * state + rb[i * 2 + k].astype(F32)
        for r in range(1, 4):
            b2(r, k).start()

    def take_forward(k):
        for r in range(1, 4):
            f1(r, k).wait_recv()
        row_forward(k)

    def take_backward(k):
        for r in range(1, 4):
            b1(r, k).wait_recv()
        row_backward(k)

    def order_in(p):
        r = p % 4
        k = p // 4
        return r, k, ((x + 4 - r) % 4) * 2 + k

    def out_copy(q):
        return pltpu.make_async_copy(sx.at[q], out_hbm.at[:, lanes_of(q)], out_sem.at[0, q])

    def gp_copy(q):
        lanes = lanes_of(q)
        return pltpu.make_async_copy(gs.at[:, lanes], gp_hbm.at[:, lanes], out_sem.at[1, q])

    def enter_forward(p, carry):
        r, k, q = order_in(p)

        @pl.when(r > 0)
        def _():
            f2(r, k).wait_recv()

        start = inf[q]
        base = start.astype(F32)
        total = None
        for b in range(NB):
            if b > 0:
                tot_b = tot[q, pl.ds(b - 1, 1), :]
                total = tot_b if b == 1 else total + tot_b
                start = (ls[q, b - 1] + jnp.exp(total) * base).astype(BF)
            carried = growth[q, blk(b), :] * dot(act_c[blk(b), :], start)
            sx[q, blk(b), :] = (acc_o[q, blk(b), :] + carried).astype(BF)
            grad_c[blk(b), :] += dot_nt(gw[q, blk(b), :], start)
        out_copy(q).start()
        return carry

    take_forward(0)
    lax.fori_loop(0, 3, intra, 0)
    take_forward(1)
    lax.fori_loop(3, 6, intra, 0)
    finish_forward(0)
    take_backward(0)
    lax.fori_loop(6, 7, intra, 0)
    finish_forward(1)
    take_backward(1)
    lax.fori_loop(7, NQ, intra, 0)
    finish_backward(0)
    lax.fori_loop(0, 4, enter_forward, 0)
    finish_backward(1)
    lax.fori_loop(4, NQ, enter_forward, 0)

    tail = pl.ds(T, HALO)

    def ghalo(src, dst, slot):
        return remote(src, dst, ghalo_s.at[slot], ghalo_r.at[slot], prv)

    def ghalo_x(q):
        return ghalo(gs.at[head, lanes_of(q)], gh.at[q], q)

    def ghalo_b():
        return ghalo(gpb.at[head], gpb.at[tail], NQ)

    def ghalo_c():
        return ghalo(gpc.at[head], gpc.at[tail], NQ + 1)

    def send_halo(copy):
        @pl.when(me > 0)
        def _():
            copy.start()

    def take_halo(copy, dst):
        @pl.when(me < 15)
        def _():
            copy.wait_recv()

        @pl.when(me == 15)
        def _():
            dst[...] = jnp.zeros((HALO, W), BF)

    def enter_backward(p, carry):
        r, k, q = order_in(p)

        @pl.when(r > 0)
        def _():
            b2(r, k).wait_recv()

        base = inb[q].astype(F32)
        totals = [None] * NB
        for b in reversed(range(NB - 1)):
            tot_b = tot[q, pl.ds(b + 1, 1), :]
            totals[b] = tot_b if b == NB - 2 else totals[b + 1] + tot_b
        for b in range(NB):
            if b < NB - 1:
                after = (la[q, b] + jnp.exp(totals[b]) * base).astype(BF)
            else:
                after = inb[q]
            outer = stte[q, blk(b), :] * dot(act_b[blk(b), :], after)
            grads = (acc_g[q, blk(b), :] + outer) * slope[q, blk(b), :]
            gs[blk(b), lanes_of(q)] = grads.astype(BF)
            if b == 0:
                send_halo(ghalo_x(q))
            grad_b[blk(b), :] += dot_nt(wx[q, blk(b), :], after)
        gp_copy(q).start()
        return carry

    for b in range(NB):
        pair_sum = ps[b] * lower_f
        pair_t = jnp.transpose(pair_sum).astype(BF)
        grad_b[blk(b), :] = dot(pair_t, act_c[blk(b), :])
        into_c = grad_c[blk(b), :] + dot(pair_sum.astype(BF), act_b[blk(b), :])
        gpc[blk(b), :] = (into_c * slope_c[blk(b), :]).astype(BF)
    send_halo(ghalo_c())
    gpc_out[pl.ds(0, T), :] = gpc[pl.ds(0, T), :]

    lax.fori_loop(0, NQ, enter_backward, 0)

    gpb[blk(0), :] = (grad_b[blk(0), :] * slope_b[blk(0), :]).astype(BF)
    send_halo(ghalo_b())
    for b in range(1, NB):
        gpb[blk(b), :] = (grad_b[blk(b), :] * slope_b[blk(b), :]).astype(BF)
    gpb_out[pl.ds(0, T), :] = gpb[pl.ds(0, T), :]
    for q in range(NQ):
        take_halo(ghalo_x(q), gh.at[q])
        gh_out[:, q * W : (q + 1) * W] = gh[q]
    for ref, out, copy in ((gpb, gpb_out, ghalo_b()), (gpc, gpc_out, ghalo_c())):
        take_halo(copy, ref.at[tail])
        out[tail, :] = ref[tail, :]

    for q in range(NQ):
        out_copy(q).wait()
        gp_copy(q).wait()

    @pl.when(me < 15)
    def _():
        for h in halos:
            h.wait_send()

    @pl.when(me > 0)
    def _():
        for q in range(NQ):
            ghalo_x(q).wait_send()
        ghalo_b().wait_send()
        ghalo_c().wait_send()

    for k in range(2):
        for r in range(1, 4):
            f1(r, k).wait_send()
            b1(r, k).wait_send()
            f2(r, k).wait_send()
            b2(r, k).wait_send()

            @pl.when(y + r <= 3)
            def _():
                yf_cp(r, k).wait_send()

            @pl.when(y - (4 - r) >= 0)
            def _():
                yb_cp(r, k).wait_send()


def back_kernel(
    out_hbm, gp_hbm, gh_hbm, gpb_hbm, gpc_hbm, kx, kb, kc, out_ref, gx_ref, gb_ref, gc_ref,
    out_v, gp_v, gx_v, gpb, gpc, gb_v, gc_v, in_sem, out_sem,
):
    def rows(i):
        return pl.ds(i * BLOCK, BLOCK)

    loads = [pltpu.make_async_copy(gh_hbm, gp_v.at[pl.ds(T, HALO)], in_sem.at[2 * NB])]
    for i in reversed(range(NB)):
        loads.append(pltpu.make_async_copy(gp_hbm.at[rows(i)], gp_v.at[rows(i)], in_sem.at[i]))
    loads.append(pltpu.make_async_copy(gpb_hbm, gpb, in_sem.at[2 * NB + 1]))
    loads.append(pltpu.make_async_copy(gpc_hbm, gpc, in_sem.at[2 * NB + 2]))
    passed = [
        pltpu.make_async_copy(out_hbm.at[rows(i)], out_v.at[rows(i)], in_sem.at[NB + i])
        for i in range(NB)
    ]
    for copy in loads + passed:
        copy.start()

    def back(value, taps, count):
        value = value.astype(F32)
        size = value.shape[0]
        grad = taps[3:4] * value[:count]
        for k in range(3):
            grad = grad + taps[k : k + 1] * pltpu.roll(value, size - (3 - k), 0)[:count]
        return grad.astype(BF)

    stores = []

    def store(src, dst, slot):
        stores.append(pltpu.make_async_copy(src, dst, out_sem.at[slot]))
        stores[-1].start()

    loads[0].wait()
    for i in reversed(range(NB)):
        loads[NB - i].wait()

        def slab(q, carry):
            lanes = pl.ds(pl.multiple_of(q * W, W), W)
            value = gp_v[pl.ds(i * BLOCK, BLOCK + HALO), lanes]
            gx_v[rows(i), lanes] = back(value, kx[:, lanes], BLOCK)
            return carry

        lax.fori_loop(0, NQ, slab, 0)
        store(gx_v.at[rows(i)], gx_ref.at[rows(i)], i)
        if i % 2 == 1:
            for j in (i - 1, i):
                passed[j].wait()
                store(out_v.at[rows(j)], out_ref.at[rows(j)], NB + j)
    loads[NB + 1].wait()
    gb_v[...] = back(gpb[...], kb[...], T)
    store(gb_v, gb_ref, 2 * NB)
    loads[NB + 2].wait()
    gc_v[...] = back(gpc[...], kc[...], T)
    store(gc_v, gc_ref, 2 * NB + 1)
    for copy in stores:
        copy.wait()


def on_device(x, b, c, kx, kb, kc, step, dlog, skip, g):
    hbm = pl.BlockSpec(memory_space=pl.ANY)
    vmem = pl.BlockSpec(memory_space=pltpu.VMEM)
    dma = pltpu.SemaphoreType.DMA
    full = (NQ, T, W)
    scratch = [
        pltpu.VMEM((T + HALO, NQ * W), BF),
        pltpu.VMEM((T + HALO, ST), BF),
        pltpu.VMEM((T + HALO, ST), BF),
        pltpu.VMEM((T, NQ * W), BF),
        pltpu.VMEM((T + 16, 6 * H), BF),
        pltpu.VMEM((NQ, 8, T), F32),
        pltpu.VMEM((T + 16, 2 * W), F32),
        pltpu.VMEM((NQ, 8, W), F32),
        pltpu.VMEM((NQ, 8, W), F32),
        pltpu.VMEM(full, F32),
        pltpu.VMEM(full, F32),
        pltpu.VMEM(full, F32),
        pltpu.VMEM(full, F32),
        pltpu.VMEM(full, F32),
        pltpu.VMEM(full, BF),
        pltpu.VMEM(full, BF),
        pltpu.VMEM(full, BF),
        pltpu.VMEM((NQ, 3, ST, W), F32),
        pltpu.VMEM((NQ, 3, ST, W), F32),
        pltpu.VMEM((NQ, HALO, W), BF),
        pltpu.VMEM((T + HALO, ST), BF),
        pltpu.VMEM((T + HALO, ST), BF),
        pltpu.VMEM((T, ST), BF),
        pltpu.VMEM((T, ST), BF),
        pltpu.VMEM((NB, ST, BLOCK), BF),
        pltpu.VMEM((NB, ST, BLOCK), BF),
        pltpu.VMEM((T, ST), F32),
        pltpu.VMEM((T, ST), F32),
        pltpu.VMEM((NB, BLOCK, BLOCK), F32),
        pltpu.VMEM((NB, BLOCK, BLOCK), F32),
        pltpu.VMEM((NB, BLOCK, BLOCK), F32),
        pltpu.VMEM((T, ST), F32),
        pltpu.VMEM((T, ST), F32),
        pltpu.VMEM((NQ, LROWS, W), BF),
        pltpu.VMEM((NQ, ST, W), BF),
        pltpu.VMEM((NQ, LROWS, W), BF),
        pltpu.VMEM((NQ, ST, W), BF),
        pltpu.VMEM((2, LROWS, W), BF),
        pltpu.VMEM((2, LROWS, W), BF),
        pltpu.VMEM((NQ, LROWS, W), BF),
        pltpu.VMEM((NQ, LROWS, W), BF),
        pltpu.VMEM((NQ, ST, W), BF),
        pltpu.VMEM((NQ, ST, W), BF),
        pltpu.VMEM((NQ, ST, W), BF),
        pltpu.VMEM((NQ, ST, W), BF),
        pltpu.VMEM((2, ST, W), F32),
        pltpu.VMEM((2, ST, W), F32),
        dma((4,)), dma((2, NQ)), dma((3,)), dma((3,)), dma((10,)), dma((10,)),
    ] + [dma((4, 2))] * 12
    out, gp, gh, gpb, gpc = pl.pallas_call(
        kernel,
        out_shape=(
            jax.ShapeDtypeStruct(x.shape, BF),
            jax.ShapeDtypeStruct(x.shape, BF),
            jax.ShapeDtypeStruct((HALO, NQ * W), BF),
            jax.ShapeDtypeStruct((T + HALO, ST), BF),
            jax.ShapeDtypeStruct((T + HALO, ST), BF),
        ),
        in_specs=[hbm] * 3 + [vmem] * 6 + [hbm],
        out_specs=(hbm, hbm, vmem, vmem, vmem),
        scratch_shapes=scratch,
        compiler_params=pltpu.CompilerParams(
            collective_id=0, has_side_effects=True, vmem_limit_bytes=67043328
        ),
    )(x, b, c, kx, kb, kc, step.T, dlog.reshape(1, H), skip.reshape(1, H), g)
    return pl.pallas_call(
        back_kernel,
        out_shape=(
            jax.ShapeDtypeStruct(x.shape, BF),
            jax.ShapeDtypeStruct(x.shape, BF),
            jax.ShapeDtypeStruct(b.shape, BF),
            jax.ShapeDtypeStruct(c.shape, BF),
        ),
        in_specs=[hbm] * 5 + [vmem] * 3,
        out_specs=(hbm,) * 4,
        scratch_shapes=[
            pltpu.VMEM((T, NQ * W), BF),
            pltpu.VMEM((T + HALO, NQ * W), BF),
            pltpu.VMEM((T, NQ * W), BF),
            pltpu.VMEM((T + HALO, ST), BF),
            pltpu.VMEM((T + HALO, ST), BF),
            pltpu.VMEM((T, ST), BF),
            pltpu.VMEM((T, ST), BF),
            dma((2 * NB + 3,)),
            dma((2 * NB + 2,)),
        ],
    )(out, gp, gh, gpb, gpc, kx, kb, kc)


def solution(mesh):
    rows = P(("doc", "context"), "head")
    taps = P(None, "head")
    return jax.shard_map(
        on_device,
        mesh=mesh,
        in_specs=(rows, rows, rows, taps, taps, taps, rows, P("head"), P("head"), rows),
        out_specs=(rows, rows, rows, rows),
        check_vma=False,
    )
```
